32 devices in a mesh: fn: 32 (over z, y, x, core).
Axes of the slice: x: 2, y: 2, z: 4, core: 2. Of those that a mesh axis runs over, the one named last changes fastest.
Arguments:
- support_functions: float32 [96, 64, 2048], P('fn'), may hold values from -50 to 50
- owner_counts: int32 [32], replicated, may hold values from 1 to 3, as said below
- region_shift: int32 [96], P('fn'), may hold values from 0 to 63
- kernel: float32 [64, 64], replicated, may hold values from -0.75 to 0.75
- external: float32 [131072], P('fn'), may hold values from -1 to 1
- kinetic_taps: float32 [15], replicated, may hold values from -3 to 3
- magic_taps: float32 [16], replicated, may hold values from -0.6 to 1.6
Outputs:
- filtered: float32 [64, 64, 2048], P('fn')
The draws below stay inside these ranges and needn't reach their ends.
Inputs may be any that keep to these rules, and one draw needn't show every extreme that they name: `owner_counts`: each owner's number of live slots; owners 2k and 2k+1 together hold exactly 4 live slots, so the counts sum to 64; slots at or past an owner's count hold no function.
All inputs are finite; a program needn't handle non-finite values.
Results may differ from the reference program's by a relative error of at most 0.0003.
Values sent between devices are 32-bit elements; how exact they have to be, the bound alone decides.
A program may use at most 64 MiB of HBM per device.

```python
import jax
import jax.numpy as jnp
from jax import lax

NX = 64
NY = 64
NZ = 32
KIN_HALF = 15
MAGIC = 16
CHEB = 1
FN_DEV = 2
SLOTS = 3
NF = 64
G = 131072
N_FN = 32


def draw_support_functions(key, part):
    first, second, third = jax.random.split(jax.random.fold_in(key, 17), 3)
    shape = (N_FN * SLOTS, NX, NY * NZ)
    base = jnp.clip(jax.random.normal(first, shape, jnp.float32), -5.0, 5.0)
    spread = jnp.log(10.0)
    lowest = 0.3162
    cell_scale = lowest * jnp.exp(jax.random.uniform(second, (1, NX, NY * NZ), jnp.float32, 0.0, spread))
    slot_scale = jnp.exp(jax.random.uniform(third, (N_FN * SLOTS, 1, 1), jnp.float32, 0.0, jnp.log(3.0)))
    return base * cell_scale * slot_scale


def draw_owner_counts(key, part):
    first, second = jax.random.split(jax.random.fold_in(key, 29), 2)
    pair_count = N_FN // 2
    spare = FN_DEV // 2
    moved = jax.random.randint(first, (pair_count,), -spare, spare + 1)
    forced = jax.random.randint(second, (), 0, pair_count)
    moved = jnp.where(jnp.arange(pair_count) == forced, spare, moved)
    paired = jnp.stack([FN_DEV + moved, FN_DEV - moved], axis=1)
    return paired.reshape(N_FN).astype(jnp.int32)


def draw_magic_taps(key, part):
    first, second = jax.random.split(jax.random.fold_in(key, 41), 2)
    tails = jnp.clip(jax.random.normal(first, (MAGIC,), jnp.float32) * 0.15, -0.5, 0.5)
    center = jax.random.uniform(second, (), jnp.float32, 0.8, 1.1)
    taps = jnp.where(jnp.arange(MAGIC) == MAGIC // 2, center, tails)
    return taps.astype(jnp.float32)


def plant(array, own_key, low, high):
    extent = array.shape
    place = [jax.random.randint(jax.random.fold_in(own_key, axis), (), 0, extent[axis]) for axis in range(len(extent))]
    array = array.at[tuple(place)].set(low)
    longest = extent.index(max(extent))
    place[longest] = (place[longest] + 1) % extent[longest]
    return array.at[tuple(place)].set(high)


def level_of(key, dims, cuts, smallest, high):
    def one(dim, parts):
        heights = jax.random.uniform(jax.random.fold_in(jax.random.fold_in(key, 6), dim), (parts,), jnp.float32, smallest / len(cuts), high / len(cuts))
        return jnp.repeat(jnp.exp(heights), dims[dim] // parts).reshape((-1,) + (1,) * (len(dims) - dim - 1))

    loudness = one(*cuts[0])
    for cut in cuts[1:]:
        loudness = loudness * one(*cut)
    return loudness


def gaussian(rng, extent, width, limit, held_as=jnp.bfloat16):
    entries = width * jax.random.normal(rng, extent, jnp.float32)
    return jnp.clip(entries, min=-limit, max=limit).astype(held_as)


def setup_inputs(seed: int = 0) -> dict:
    keys = jax.random.split(jax.random.key(seed), 8)
    support_functions = draw_support_functions(jax.random.fold_in(keys[7], 71), 0)
    owner_counts = draw_owner_counts(jax.random.fold_in(keys[7], 71), 0)
    region_shift = plant(jax.random.randint(keys[2], (N_FN * SLOTS,), 0, NX), jax.random.fold_in(keys[2], 1), 0, NX - 1).astype(jnp.int32)
    kernel = gaussian(keys[3], (NF, NF), NF ** -0.5, 0.75, jnp.float32)
    external = jnp.clip(jax.random.uniform(keys[4], (G,), jnp.float32, -1.0, 1.0) * level_of(keys[4], (G,), ((0, 32),), -0.4, 0.0), -1.0, 1.0)
    kinetic_taps = gaussian(keys[5], (KIN_HALF,), 0.3, 3.0, jnp.float32)
    magic_taps = draw_magic_taps(jax.random.fold_in(keys[7], 71), 0)
    return dict(support_functions=support_functions, owner_counts=owner_counts, region_shift=region_shift, kernel=kernel, external=external, kinetic_taps=kinetic_taps, magic_taps=magic_taps)


precise = lax.Precision.HIGHEST


def roll_rows(slab_rows, shift):
    length = slab_rows.shape[0]
    doubled = jnp.concatenate([slab_rows, slab_rows], axis=0)
    start_row = ((length - shift) % length).astype(jnp.int32)
    return lax.dynamic_slice_in_dim(doubled, start_row, length, 0)


def circulant(filter_taps, length):
    center = filter_taps.shape[0] // 2
    row_index = jnp.arange(length)[:, None]
    col_index = jnp.arange(length)[None, :]
    summed = jnp.zeros((length, length), filter_taps.dtype)
    for position in range(filter_taps.shape[0]):
        matches = col_index == (row_index + position - center) % length
        summed = summed + jnp.where(matches, filter_taps[position], 0.0)
    return summed


def along(matrix, values, axis_number):
    if axis_number == 1:
        return jnp.einsum("ik,fkyz->fiyz", matrix, values, precision=precise)
    if axis_number == 2:
        return jnp.einsum("ik,fxkz->fxiz", matrix, values, precision=precise)
    return jnp.einsum("ik,fxyk->fxyi", matrix, values, precision=precise)


def full_kinetic(kinetic_taps):
    return jnp.concatenate([kinetic_taps[::-1], kinetic_taps[1:]])


def potentials(mixed_rows, external):
    half = mixed_rows.shape[0] // 2
    rho_up = jnp.mean(mixed_rows[:half] ** 2, axis=0)
    rho_down = jnp.mean(mixed_rows[half:] ** 2, axis=0)
    summed = 0.5 * (rho_up + rho_down)
    spin_up = external + summed - jnp.cbrt(6.0 / jnp.pi * rho_up + 1e-6)
    spin_down = external + summed - jnp.cbrt(6.0 / jnp.pi * rho_down + 1e-6)
    return jnp.stack([spin_up, spin_down])


def spectral_bound(kinetic_taps, potential_rows):
    return 1.0 + 1.5 * jnp.sum(jnp.abs(full_kinetic(kinetic_taps))) + jnp.max(jnp.abs(potential_rows))


def chebyshev(field_rows, spin_potential, kinetic_taps, magic_taps, spectral):
    kinetic_full = full_kinetic(kinetic_taps)
    magic_norm = magic_taps / jnp.sum(jnp.abs(magic_taps))
    sizes_xyz = field_rows.shape[1:]
    kinetic_mats = [circulant(kinetic_full, sizes_xyz[index]) for index in range(3)]
    magic_mats = [circulant(magic_norm, sizes_xyz[index]) for index in range(3)]

    def apply_scaled(values):
        kinetic = along(kinetic_mats[0], values, 1) + along(kinetic_mats[1], values, 2) + along(kinetic_mats[2], values, 3)
        smooth = along(magic_mats[2], along(magic_mats[1], along(magic_mats[0], values, 1), 2), 3)
        weighted = spin_potential * smooth
        back = along(magic_mats[0].T, along(magic_mats[1].T, along(magic_mats[2].T, weighted, 3), 2), 1)
        return (-0.5 * kinetic + back) / spectral

    previous = field_rows
    current = apply_scaled(field_rows)
    for iteration in range(CHEB - 1):
        following = 2.0 * apply_scaled(current) - previous
        previous = current
        current = following
    return current


def reference(support_functions, owner_counts, region_shift, kernel, external, kinetic_taps, magic_taps):
    slot_total = support_functions.shape[0]
    slot_each = slot_total // N_FN
    rolled = jax.vmap(roll_rows)(support_functions, region_shift).reshape(slot_total, -1)
    starts = jnp.cumsum(owner_counts) - owner_counts
    slot_ids = jnp.arange(slot_total)
    owners = slot_ids // slot_each
    within = slot_ids % slot_each
    global_index = (starts[owners] + within).astype(jnp.int32)
    live_slot = within < owner_counts[owners]
    columns = jnp.where(live_slot[None, :], jnp.take(kernel, jnp.clip(global_index, 0, NF - 1), axis=1), 0.0)
    mixed_rows = jnp.dot(columns, rolled, precision=precise, preferred_element_type=jnp.float32)
    potential_rows = potentials(mixed_rows, external)
    spectral = spectral_bound(kinetic_taps, potential_rows)
    half = NF // 2
    results = []
    for spin in range(2):
        field_rows = mixed_rows[spin * half:(spin + 1) * half].reshape(half, NX, NY, NZ)
        spin_potential = potential_rows[spin].reshape(1, NX, NY, NZ)
        results.append(chebyshev(field_rows, spin_potential, kinetic_taps, magic_taps, spectral))
    return jnp.concatenate(results, axis=0).reshape(NF, NX, NY * NZ)
```

```python
import functools

import jax
import jax.numpy as jnp
from jax import lax
from jax.experimental import pallas as pl
from jax.experimental.pallas import tpu as pltpu
from jax.sharding import PartitionSpec as P

NY = 64
NZ = 32
LANES = 128
SLAB = 256
YS = SLAB // NZ
GROUP = 4
VMEM = pl.BlockSpec(memory_space=pltpu.VMEM)
SMEM = pl.BlockSpec(memory_space=pltpu.SMEM)
HBM = pl.BlockSpec(memory_space=pltpu.HBM)
F32 = jnp.float32
BF16 = jnp.bfloat16


def halves(values):
    high = values.astype(BF16)
    low = (values - high.astype(F32)).astype(BF16)
    return high, low


def dot(left, right):
    return jnp.dot(left, right, preferred_element_type=F32)


def params(**more):
    return pltpu.CompilerParams(vmem_limit_bytes=48 << 20, has_side_effects="collective_id" in more, **more)


def x_of(row, devices, spread):
    if spread == 1:
        return row
    return lax.rem(row, devices) * spread + row // devices


def matrices(devices, kin_ref, mag_ref, xf_ref, xb_ref, kin_out, fwd_out, bwd_out):
    nx = xb_ref.shape[0]
    kin_half = kin_ref.shape[0]
    taps = mag_ref.shape[0]
    kin_count = 2 * kin_half - 1
    kin_center, mag_center = kin_count // 2, taps // 2
    kin = [-0.5 * kin_ref[abs(t - kin_center)] for t in range(kin_count)]
    mag = [mag_ref[t] for t in range(taps)]
    total = functools.reduce(lambda a, b: a + b, [jnp.abs(m) for m in mag])

    def picked(index, values, first=0):
        summed = jnp.zeros(index.shape, F32)
        for t, value in enumerate(values):
            summed = jnp.where(index == t + first, value, summed)
        return summed

    def iota(shape, dim):
        return lax.broadcasted_iota(jnp.int32, shape, dim)

    spread = max(nx // devices, 1)
    out_x, in_x = (x_of(iota((nx, nx), d), devices, spread) for d in (0, 1))
    ahead = lax.rem(in_x - out_x + mag_center + nx, nx)
    behind = lax.rem(out_x - in_x + mag_center + nx, nx)
    across = lax.rem(in_x - out_x + kin_center + nx, nx)
    fh, fl = halves(picked(ahead, mag) / total)
    kh, kl = halves(picked(across, kin))
    bh, bl = halves(picked(behind, mag) / total)
    xf_ref[:nx] = jnp.concatenate([fh, fl, fh], axis=1)
    xf_ref[nx:] = jnp.concatenate([kh, kl, kh], axis=1)
    xb_ref[...] = jnp.concatenate([bh, bl, bh], axis=1)

    square = (SLAB, SLAB)
    row, col = iota(square, 0), iota(square, 1)
    in_y, in_z = row // NZ, lax.rem(row, NZ)
    out_y, out_z = col // NZ, lax.rem(col, NZ)
    dy, dz = in_y - out_y, in_z - out_z

    def along_y(delta, values, center, d):
        low = max(YS * d + center - (YS - 1), 0)
        high = min(YS * d + center + YS - 1, len(values) - 1)
        return picked(delta + (YS * d + center), values[low:high + 1], low)

    mag_z = picked(lax.rem(dz + mag_center + NZ, NZ), mag) / total
    mag_zt = picked(lax.rem(mag_center - dz + NZ, NZ), mag) / total
    kin_z = picked(lax.rem(dz + kin_center + NZ, NZ), kin)
    reach = fwd_out.shape[0] // 2 // SLAB // 2
    kin_reach = kin_out.shape[0] // 2 // SLAB // 2
    for n in range(2 * reach + 1):
        d = n - reach
        for out, y_part, z_part in (
            (fwd_out, along_y(dy, mag, mag_center, d), mag_z),
            (bwd_out, along_y(-dy, mag, mag_center, -d), mag_zt),
        ):
            high, low = halves(y_part / total * z_part)
            out[n * SLAB:(n + 1) * SLAB] = high
            base = (2 * reach + 1 + n) * SLAB
            out[base:base + SLAB] = low
    for n in range(2 * kin_reach + 1):
        d = n - kin_reach
        value = jnp.where(dz == 0, along_y(dy, kin, kin_center, d), 0.0)
        if d == 0:
            value = value + jnp.where(dy == 0, kin_z, 0.0)
        high, low = halves(value)
        kin_out[n * SLAB:(n + 1) * SLAB] = high
        base = (2 * kin_reach + 1 + n) * SLAB
        kin_out[base:base + SLAB] = low


def mixing_matrix(devices, counts_ref, kernel_ref, mix_out):
    functions = kernel_ref.shape[0]
    local = functions // devices
    full = (functions, functions)
    row, col = (lax.broadcasted_iota(jnp.int32, full, d) for d in (0, 1))
    lead = jnp.zeros((1, functions), jnp.int32)
    lane = lax.broadcasted_iota(jnp.int32, (1, functions), 1)
    pair = lane // (2 * local)
    for k in range(devices // 2):
        lead = jnp.where(pair == k, counts_ref[2 * k], lead)
    slot = lax.rem(lane, local)
    odd = lax.rem(lane // local, 2) == 1
    count = jnp.where(odd, 2 * local - lead, lead)
    first = jnp.where(odd, lead, 0)
    stand_in = jnp.where(odd, local, 2 * local - 1)
    second = jnp.where(count < local, stand_in, first + 1)
    place = pair * (2 * local) + jnp.where(slot == 0, first, second)
    wanted = lax.rem(row, devices) * local + row // devices
    row_pick = jnp.where(wanted == col, 1.0, 0.0).astype(BF16)
    col_pick = jnp.where(row == place, 1.0, 0.0).astype(BF16)
    parts = [dot(dot(row_pick, part).astype(BF16), col_pick).astype(BF16) for part in halves(kernel_ref[...])]
    mix_out[...] = jnp.concatenate([parts[0], parts[1], parts[0]], axis=1)


def partner(me, k):
    bit = 1
    there = me
    while bit <= k:
        if k & bit:
            there = there + bit - 2 * bit * ((me // bit) % 2)
        bit *= 2
    return there


def far_first(devices):
    half = devices // 2
    order = []
    for n in range(half):
        order += [half + n, n]
    return [k for k in order if k]


def remote(source, target, send, recv, device):
    return pltpu.make_async_remote_copy(
        src_ref=source, dst_ref=target, send_sem=send, recv_sem=recv,
        device_id=(device,), device_id_type=pl.DeviceIdType.MESH,
    )


def cube_root(x):
    guess = jnp.exp(jnp.log(x) * (1.0 / 3.0))
    return guess - (guess - x / (guess * guess)) * (1.0 / 3.0)


def exchange_kernel(devices, parts,
                    slots_hbm, shift_hbm, counts_hbm, kernel_hbm, external_hbm, kin_hbm, mag_hbm,
                    xf_ref, xb_ref, kin_out, fwd_out, bwd_out, back_ref, gpot_ref,
                    raw_ref, own_ref, out_ref, in_ref, got_ref, mixed_ref, pots_ref,
                    mix_ref, kernel_ref, external_ref, up_ref, down_ref,
                    shift_ref, counts_ref, kin_ref, mag_ref,
                    load_sem, swap_sem, lead_send, lead_recv, part_send, part_recv,
                    back_send, back_recv, pot_send, pot_recv):
    slot_each, nx, cells = raw_ref.shape
    functions = kernel_ref.shape[0]
    local = functions // devices
    q_count = cells // LANES
    rows_per = external_ref.shape[0]
    rows = rows_per // parts
    half = devices // 2
    count = functions // 2
    me = lax.axis_index("fn")
    side = me // half
    across = partner(me, half)
    mate = partner(me, 1)

    def load(source, target, k):
        copy = pltpu.make_async_copy(source, target, load_sem.at[k])
        copy.start()
        return copy

    slot_loads = {0: load(slots_hbm.at[0], raw_ref.at[0], 0)}
    shift_load = load(shift_hbm, shift_ref, slot_each)
    for s in reversed(range(1, slot_each)):
        slot_loads[s] = load(slots_hbm.at[s], raw_ref.at[s], s)
    small = [load(a, b, slot_each + 1 + k) for k, (a, b) in enumerate((
        (counts_hbm, counts_ref), (kernel_hbm, kernel_ref), (external_hbm, external_ref),
        (kin_hbm, kin_ref), (mag_hbm, mag_ref),
    ))]

    barrier = pltpu.get_barrier_semaphore()
    for k in range(1, devices):
        pl.semaphore_signal(barrier, inc=1, device_id=(partner(me, k),), device_id_type=pl.DeviceIdType.MESH)
    order = far_first(devices)

    def block(part, device, field=0):
        return pl.multiple_of(((part * devices + device) * local + field) * rows, 8)

    spread = max(rows_per // q_count, 1)
    x_row = lax.broadcasted_iota(jnp.int32, (nx, nx), 0)
    x_col = lax.broadcasted_iota(jnp.int32, (nx, nx), 1)
    x_row = x_of(x_row, devices, spread)

    def rolled(s, target, fields, field):
        picked = lax.rem(x_row - shift_ref[s] + nx, nx) == x_col
        pick = jnp.where(picked, 1.0, 0.0).astype(BF16)
        pick = jnp.concatenate([pick, pick], axis=1)
        slot_loads[s].wait()
        for h in range(cells // SLAB):
            high, low = halves(raw_ref[s, :, h * SLAB:(h + 1) * SLAB])
            moved = dot(pick, jnp.concatenate([high, low], axis=0))
            for k in range(SLAB // LANES):
                q = h * (SLAB // LANES) + k
                column = moved[:, k * LANES:(k + 1) * LANES]
                if rows_per >= q_count:
                    for xo in range(spread):
                        at = xo * q_count + q
                        start = (at // rows * devices * fields + field) * rows + at % rows
                        target[pl.ds(start, devices, stride=fields * rows), :] = (
                            column[xo * devices:(xo + 1) * devices]
                        )
                else:
                    start = (q // rows * fields + field) * rows + q % rows
                    target[pl.ds(start, nx, stride=q_count // rows * fields * rows), :] = column

    shift_load.wait()
    rolled(0, own_ref, local, 0)
    pl.semaphore_wait(barrier, devices - 1)

    sends = []
    arrivals = [[] for _ in range(parts)]

    def give(part, first, fields, k, send, recv):
        there = partner(me, k)
        copy = remote(own_ref.at[pl.ds(block(part, there, first), fields * rows)],
                      got_ref.at[pl.ds(block(part, me, first), fields * rows)], send.at[k], recv.at[k], there)
        copy.start()
        sends.append(copy)
        arrivals[part].append(copy)

    for k in order:
        give(0, 0, 1, k, lead_send, lead_recv)
    last = slot_each - 1
    rolled(last, out_ref, 1, 0)
    swap = remote(out_ref, in_ref, swap_sem.at[0], swap_sem.at[1], mate)
    swap.start()
    rolled(1, own_ref, local, 1)
    for copy in small:
        copy.wait()
    swap.wait_recv()
    lone = jnp.full((rows, LANES), counts_ref[me], jnp.int32) < local
    for part in range(parts):
        for dest in range(devices):
            where = ((part * devices + dest) * local + 1) * rows
            there = (part * devices + dest) * rows
            mine = own_ref[where:where + rows, :]
            own_ref[where:where + rows, :] = jnp.where(lone, in_ref[there:there + rows, :], mine)
    for k in order:
        give(0, 1, local - 1, k, part_send.at[0], part_recv.at[0])
    for part in range(1, parts):
        for k in order:
            give(part, 0, local, k, part_send.at[part], part_recv.at[part])
    for part in range(parts):
        got_ref[pl.ds(block(part, me), local * rows), :] = own_ref[pl.ds(block(part, me), local * rows), :]

    mixing_matrix(devices, counts_ref, kernel_ref, mix_ref)
    matrices(devices, kin_ref, mag_ref, xf_ref, xb_ref, kin_out, fwd_out, bwd_out)

    def mix(part):
        base = part * functions * rows
        for c in range(0, rows, 2):
            values = jnp.concatenate(
                [got_ref[pl.ds(base + c + k, functions, stride=rows), :] for k in range(2)], axis=1
            )
            high, low = halves(values)
            mixed = dot(mix_ref[...], jnp.concatenate([high, high, low], axis=0))
            up = down = 0.0
            for j in range(local):
                piece = mixed[j * devices:(j + 1) * devices]
                for k in range(2):
                    mixed_ref[pl.ds(base + j * rows + c + k, devices, stride=local * rows), :] = (
                        piece[:, k * LANES:(k + 1) * LANES]
                    )
                squared = piece * piece
                up = up + jnp.sum(squared[:half], axis=0, keepdims=True)
                down = down + jnp.sum(squared[half:], axis=0, keepdims=True)
            for k in range(2):
                up_ref[c + k:c + k + 1, :] = up[:, k * LANES:(k + 1) * LANES]
                down_ref[c + k:c + k + 1, :] = down[:, k * LANES:(k + 1) * LANES]
        rho_up, rho_down = up_ref[...] / count, down_ref[...] / count
        shared = external_ref[part * rows:(part + 1) * rows, :] + 0.5 * (rho_up + rho_down)
        spins = [shared - cube_root((6.0 / jnp.pi) * rho + 1e-6) for rho in (rho_up, rho_down)]
        for spin in range(2):
            pots_ref[spin, part * rows:(part + 1) * rows] = spins[spin]
        sizes = jnp.maximum(jnp.abs(spins[0]), jnp.abs(spins[1]))
        peak = sizes[:8]
        for w in range(1, rows // 8):
            peak = jnp.maximum(peak, sizes[w * 8:(w + 1) * 8])
        return peak

    peak = None
    returns, handed, waits = [], [], []
    for part in range(parts):
        for copy in arrivals[part]:
            copy.wait_recv()
        here = mix(part)
        peak = here if peak is None else jnp.maximum(peak, here)
        begin, extent = part * rows, rows
        if part == parts - 1:
            extent = rows + 8
            for spin in range(2):
                pots_ref[spin, rows_per:] = peak
        span = pl.ds(begin, extent)

        def show(source, owner, slot, there):
            copy = remote(source, gpot_ref.at[owner, span], pot_send.at[part, slot], pot_recv.at[part, slot], there)
            copy.start()
            return copy

        handed = show(pots_ref.at[1 - side, span], me, 0, across)
        sends.append(handed)
        for k in range(1, half):
            waits.append(show(pots_ref.at[side, span], me, k, partner(me, k)))
        for k in order:
            there = partner(me, k)
            copy = remote(mixed_ref.at[pl.ds(block(part, there), local * rows)],
                          back_ref.at[pl.ds(block(part, me), local * rows)],
                          back_send.at[part, k], back_recv.at[part, k], there)
            copy.start()
            returns.append(copy)
        back_ref[pl.ds(block(part, me), local * rows), :] = mixed_ref[pl.ds(block(part, me), local * rows), :]
        gpot_ref[me, begin:begin + extent] = pots_ref[side, begin:begin + extent]
        handed.wait_recv()
        for k in range(1, half):
            waits.append(show(gpot_ref.at[across, span], across, half + k, partner(me, k)))
    for copy in returns + waits:
        copy.wait_recv()
    for copy in [swap, *sends, *returns, *waits]:
        copy.wait_send()


def filter_kernel(devices, rows_per, parts, kin_ref, got_ref, gpot_ref, xf_ref, xb_ref, kinm_ref, fwd_ref, bwd_ref, out_ref,
                  v_hi, v_lo, p_hi, p_lo, w_hi, w_lo, acc_ref, pot_ref, stage_ref):
    local, nx, cells = out_ref.shape
    slabs = cells // SLAB
    q_count = cells // LANES
    per_slab = SLAB // LANES
    spread = max(rows_per // q_count, 1)

    rows = rows_per // parts
    pot_rows = gpot_ref.shape[0] // devices

    def plane(field, q):
        if field == local:
            ref, stride, extent = gpot_ref, pot_rows, rows_per
        else:
            ref, stride, extent = got_ref, local * rows, rows

        def start(x):
            if field == local:
                return x
            return (x // rows * devices * local + field) * rows + x % rows

        if rows_per >= q_count:
            return jnp.concatenate([
                ref[pl.ds(start(xo * q_count + q), devices, stride=stride), :] for xo in range(spread)
            ], axis=0)
        split = q_count // extent
        return ref[pl.ds((q // extent) * stride + start(q % extent), nx, stride=split * stride), :]

    def slab_of(field, h):
        return jnp.concatenate([plane(field, h * per_slab + k) for k in range(per_slab)], axis=1)

    for h in range(slabs):
        pot_ref[h] = slab_of(local, h)
        for f in range(local):
            high, low = halves(slab_of(f, h))
            where = slice(f * nx, (f + 1) * nx)
            v_hi[h, where] = high
            v_lo[h, where] = low
            both = dot(xf_ref[...], jnp.concatenate([high, high, low], axis=0))
            p_hi[h, where], p_lo[h, where] = halves(both[:nx])
            acc_ref[h, where] = both[nx:]

    def banded(hi_ref, lo_ref, matrix_ref, h):
        width = matrix_ref.shape[0] // 2
        count = width // SLAB

        def wide(ref):
            return jnp.concatenate([
                jnp.concatenate(
                    [ref[lax.rem(h + g + (n - count // 2) + slabs, slabs)] for n in range(count)], axis=1
                ) for g in range(GROUP)
            ], axis=0)

        high, low = wide(hi_ref), wide(lo_ref)
        return dot(high, matrix_ref[:width]) + (dot(low, matrix_ref[:width]) + dot(high, matrix_ref[width:]))

    def forward(step, carry):
        h = step * GROUP
        kinetic = banded(v_hi, v_lo, kinm_ref, h)
        smooth = banded(p_hi, p_lo, fwd_ref, h)
        for g in range(GROUP):
            base = g * local * nx
            acc_ref[h + g] += kinetic[base:base + local * nx]
            potential = pot_ref[h + g]
            for f in range(local):
                high, low = halves(smooth[base + f * nx:base + (f + 1) * nx] * potential)
                mixed = dot(xb_ref[...], jnp.concatenate([high, high, low], axis=0))
                w_hi[h + g, f * nx:(f + 1) * nx], w_lo[h + g, f * nx:(f + 1) * nx] = halves(mixed)
        return carry

    lax.fori_loop(0, slabs // GROUP, forward, 0)

    sides = jnp.abs(kin_ref[0])
    for t in range(1, kin_ref.shape[0]):
        sides = sides + 2.0 * jnp.abs(kin_ref[t])
    peaks = gpot_ref[rows_per:pot_rows, :]
    for e in range(1, devices):
        peaks = jnp.maximum(peaks, gpot_ref[e * pot_rows + rows_per:(e + 1) * pot_rows, :])
    bound = 1.0 + 1.5 * sides + jnp.max(peaks)

    def backward(step, carry):
        first = step * GROUP
        back = banded(w_hi, w_lo, bwd_ref, first)
        count = nx // spread
        for g in range(GROUP):
            h = first + g
            result = (acc_ref[h] + back[g * local * nx:(g + 1) * local * nx]) / bound
            for f in range(local):
                for k in range(per_slab):
                    q = h * per_slab + k
                    if spread > 1:
                        for xo in range(spread):
                            block = result[f * nx + xo * count:f * nx + (xo + 1) * count, k * LANES:(k + 1) * LANES]
                            stage_ref[f, q, pl.ds(xo, count, stride=spread), :] = block
                        ordered = stage_ref[f, q]
                    else:
                        ordered = result[f * nx:(f + 1) * nx, k * LANES:(k + 1) * LANES]
                    out_ref[f, :, pl.ds(pl.multiple_of(q * LANES, LANES), LANES)] = ordered
        return carry

    lax.fori_loop(0, slabs // GROUP, backward, 0)


def shaped(shape, dtype=F32):
    return jax.ShapeDtypeStruct(shape, dtype)


def body(support_functions, owner_counts, region_shift, kernel, external, kinetic_taps, magic_taps):
    devices = lax.axis_size("fn")
    slot_each, nx, cells = support_functions.shape
    functions = kernel.shape[0]
    local = functions // devices
    rows_per = nx * cells // devices // LANES
    q_count = cells // LANES
    parts = 2 if rows_per % (2 * q_count) == 0 else 1
    rows = rows_per // parts
    reach = -(-(magic_taps.shape[0] // 2) // YS)
    kin_reach = -(-(kinetic_taps.shape[0] - 1) // YS)

    each = pltpu.SemaphoreType.DMA((devices,))
    each_part = pltpu.SemaphoreType.DMA((parts, devices))
    flat = (nx * q_count, LANES)
    whole = (functions * rows_per, LANES)
    xf, xb, kin_m, fwd_m, bwd_m, back, gpot = pl.pallas_call(
        functools.partial(exchange_kernel, devices, parts),
        out_shape=(
            shaped((2 * nx, 3 * nx), BF16),
            shaped((nx, 3 * nx), BF16),
            shaped((2 * (2 * kin_reach + 1) * SLAB, SLAB), BF16),
            shaped((2 * (2 * reach + 1) * SLAB, SLAB), BF16),
            shaped((2 * (2 * reach + 1) * SLAB, SLAB), BF16),
            shaped(whole),
            shaped((devices, rows_per + 8, LANES)),
        ),
        in_specs=[HBM] * 7,
        out_specs=(VMEM,) * 7,
        scratch_shapes=[
            pltpu.VMEM((slot_each, nx, cells), F32), pltpu.VMEM(whole, F32),
            pltpu.VMEM(flat, F32), pltpu.VMEM(flat, F32), pltpu.VMEM(whole, F32), pltpu.VMEM(whole, F32),
            pltpu.VMEM((2, rows_per + 8, LANES), F32), pltpu.VMEM((functions, 3 * functions), BF16),
            pltpu.VMEM((functions, functions), F32), pltpu.VMEM((rows_per, LANES), F32),
            pltpu.VMEM((rows, LANES), F32), pltpu.VMEM((rows, LANES), F32),
            pltpu.SMEM(region_shift.shape, jnp.int32), pltpu.SMEM(owner_counts.shape, jnp.int32),
            pltpu.SMEM(kinetic_taps.shape, F32), pltpu.SMEM(magic_taps.shape, F32),
            pltpu.SemaphoreType.DMA((slot_each + 6,)), pltpu.SemaphoreType.DMA((2,)), each, each,
        ] + [each_part] * 6,
        compiler_params=params(collective_id=0),
        name="exchange",
    )(support_functions, region_shift, owner_counts, kernel, external.reshape(rows_per, LANES), kinetic_taps, magic_taps)

    slabs = cells // SLAB
    tile = (slabs, local * nx, SLAB)
    return pl.pallas_call(
        functools.partial(filter_kernel, devices, rows_per, parts),
        out_shape=shaped((local, nx, cells)),
        in_specs=[SMEM] + [VMEM] * 7,
        out_specs=VMEM,
        scratch_shapes=[pltpu.VMEM(tile, BF16)] * 6
        + [pltpu.VMEM(tile, F32), pltpu.VMEM((slabs, nx, SLAB), F32),
           pltpu.VMEM((local, cells // LANES, nx, LANES), F32)],
        compiler_params=params(),
        name="filter",
    )(kinetic_taps, back, gpot.reshape(-1, LANES), xf, xb, kin_m, fwd_m, bwd_m)


def solution(mesh):
    placed = (P("fn", None, None), P(), P("fn"), P(), P("fn"), P(), P())
    return jax.shard_map(
        body, mesh=mesh, in_specs=placed, out_specs=P("fn", None, None), check_vma=False
    )
```

```python
import functools

import jax
import jax.numpy as jnp
from jax import lax
from jax.experimental import pallas as pl
from jax.experimental.pallas import tpu as pltpu
from jax.sharding import PartitionSpec as P

NY = 64
NZ = 32
LANES = 128
SLAB = 256
YS = SLAB // NZ
GROUP = 4
VMEM = pl.BlockSpec(memory_space=pltpu.VMEM)
SMEM = pl.BlockSpec(memory_space=pltpu.SMEM)
HBM = pl.BlockSpec(memory_space=pltpu.HBM)
F32 = jnp.float32
BF16 = jnp.bfloat16


def halves(values):
    high = values.astype(BF16)
    low = (values - high.astype(F32)).astype(BF16)
    return high, low


def dot(left, right):
    return jnp.dot(left, right, preferred_element_type=F32)


def params(**more):
    return pltpu.CompilerParams(vmem_limit_bytes=48 << 20, has_side_effects="collective_id" in more, **more)


def x_of(row, devices, spread):
    if spread == 1:
        return row
    return lax.rem(row, devices) * spread + row // devices


def matrices(devices, kin_ref, mag_ref, xf_ref, xb_ref, kin_out, fwd_out, bwd_out):
    nx = xb_ref.shape[0]
    kin_half = kin_ref.shape[0]
    taps = mag_ref.shape[0]
    kin_count = 2 * kin_half - 1
    kin_center, mag_center = kin_count // 2, taps // 2
    kin = [-0.5 * kin_ref[abs(t - kin_center)] for t in range(kin_count)]
    mag = [mag_ref[t] for t in range(taps)]
    total = functools.reduce(lambda a, b: a + b, [jnp.abs(m) for m in mag])

    def picked(index, values, first=0):
        summed = jnp.zeros(index.shape, F32)
        for t, value in enumerate(values):
            summed = jnp.where(index == t + first, value, summed)
        return summed

    def iota(shape, dim):
        return lax.broadcasted_iota(jnp.int32, shape, dim)

    spread = max(nx // devices, 1)
    out_x, in_x = (x_of(iota((nx, nx), d), devices, spread) for d in (0, 1))
    ahead = lax.rem(in_x - out_x + mag_center + nx, nx)
    behind = lax.rem(out_x - in_x + mag_center + nx, nx)
    across = lax.rem(in_x - out_x + kin_center + nx, nx)
    fh, fl = halves(picked(ahead, mag) / total)
    kh, kl = halves(picked(across, kin))
    bh, bl = halves(picked(behind, mag) / total)
    xf_ref[:nx] = jnp.concatenate([fh, fl, fh], axis=1)
    xf_ref[nx:] = jnp.concatenate([kh, kl, kh], axis=1)
    xb_ref[...] = jnp.concatenate([bh, bl, bh], axis=1)

    square = (SLAB, SLAB)
    row, col = iota(square, 0), iota(square, 1)
    in_y, in_z = row // NZ, lax.rem(row, NZ)
    out_y, out_z = col // NZ, lax.rem(col, NZ)
    dy, dz = in_y - out_y, in_z - out_z

    def along_y(delta, values, center, d):
        low = max(YS * d + center - (YS - 1), 0)
        high = min(YS * d + center + YS - 1, len(values) - 1)
        return picked(delta + (YS * d + center), values[low:high + 1], low)

    mag_z = picked(lax.rem(dz + mag_center + NZ, NZ), mag) / total
    mag_zt = picked(lax.rem(mag_center - dz + NZ, NZ), mag) / total
    kin_z = picked(lax.rem(dz + kin_center + NZ, NZ), kin)
    reach = fwd_out.shape[0] // 2 // SLAB // 2
    kin_reach = kin_out.shape[0] // 2 // SLAB // 2
    for n in range(2 * reach + 1):
        d = n - reach
        for out, y_part, z_part in (
            (fwd_out, along_y(dy, mag, mag_center, d), mag_z),
            (bwd_out, along_y(-dy, mag, mag_center, -d), mag_zt),
        ):
            high, low = halves(y_part / total * z_part)
            out[n * SLAB:(n + 1) * SLAB] = high
            base = (2 * reach + 1 + n) * SLAB
            out[base:base + SLAB] = low
    for n in range(2 * kin_reach + 1):
        d = n - kin_reach
        value = jnp.where(dz == 0, along_y(dy, kin, kin_center, d), 0.0)
        if d == 0:
            value = value + jnp.where(dy == 0, kin_z, 0.0)
        high, low = halves(value)
        kin_out[n * SLAB:(n + 1) * SLAB] = high
        base = (2 * kin_reach + 1 + n) * SLAB
        kin_out[base:base + SLAB] = low


def mixing_matrix(devices, counts_ref, kernel_ref, mix_out):
    functions = kernel_ref.shape[0]
    local = functions // devices
    full = (functions, functions)
    row, col = (lax.broadcasted_iota(jnp.int32, full, d) for d in (0, 1))
    lead = jnp.zeros((1, functions), jnp.int32)
    lane = lax.broadcasted_iota(jnp.int32, (1, functions), 1)
    pair = lane // (2 * local)
    for k in range(devices // 2):
        lead = jnp.where(pair == k, counts_ref[2 * k], lead)
    slot = lax.rem(lane, local)
    odd = lax.rem(lane // local, 2) == 1
    count = jnp.where(odd, 2 * local - lead, lead)
    first = jnp.where(odd, lead, 0)
    stand_in = jnp.where(odd, local, 2 * local - 1)
    second = jnp.where(count < local, stand_in, first + 1)
    place = pair * (2 * local) + jnp.where(slot == 0, first, second)
    wanted = lax.rem(row, devices) * local + row // devices
    row_pick = jnp.where(wanted == col, 1.0, 0.0).astype(BF16)
    col_pick = jnp.where(row == place, 1.0, 0.0).astype(BF16)
    parts = [dot(dot(row_pick, part).astype(BF16), col_pick).astype(BF16) for part in halves(kernel_ref[...])]
    mix_out[...] = jnp.concatenate([parts[0], parts[1], parts[0]], axis=1)


def partner(me, k):
    bit = 1
    there = me
    while bit <= k:
        if k & bit:
            there = there + bit - 2 * bit * ((me // bit) % 2)
        bit *= 2
    return there


def far_first(devices):
    half = devices // 2
    order = []
    for n in range(half):
        order += [half + n, n]
    return [k for k in order if k]


def remote(source, target, send, recv, device):
    return pltpu.make_async_remote_copy(
        src_ref=source, dst_ref=target, send_sem=send, recv_sem=recv,
        device_id=(device,), device_id_type=pl.DeviceIdType.MESH,
    )


def cube_root(x):
    guess = jnp.exp(jnp.log(x) * (1.0 / 3.0))
    return guess - (guess - x / (guess * guess)) * (1.0 / 3.0)


def exchange_kernel(devices, parts,
                    slots_hbm, shift_hbm, counts_hbm, kernel_hbm, external_hbm, kin_hbm, mag_hbm,
                    xf_ref, xb_ref, kin_out, fwd_out, bwd_out, back_ref, gpot_ref,
                    raw_ref, own_ref, out_ref, in_ref, got_ref, mixed_ref, pots_ref,
                    mix_ref, kernel_ref, external_ref, up_ref, down_ref,
                    shift_ref, counts_ref, kin_ref, mag_ref,
                    load_sem, swap_sem, lead_send, lead_recv, part_send, part_recv,
                    back_send, back_recv, pot_send, pot_recv):
    slot_each, nx, cells = raw_ref.shape
    functions = kernel_ref.shape[0]
    local = functions // devices
    q_count = cells // LANES
    rows_per = external_ref.shape[0]
    rows = rows_per // parts
    half = devices // 2
    count = functions // 2
    me = lax.axis_index("fn")
    side = me // half
    across = partner(me, half)
    mate = partner(me, 1)

    def load(source, target, k):
        copy = pltpu.make_async_copy(source, target, load_sem.at[k])
        copy.start()
        return copy

    slot_loads = {0: load(slots_hbm.at[0], raw_ref.at[0], 0)}
    shift_load = load(shift_hbm, shift_ref, slot_each)
    for s in reversed(range(1, slot_each)):
        slot_loads[s] = load(slots_hbm.at[s], raw_ref.at[s], s)
    small = [load(a, b, slot_each + 1 + k) for k, (a, b) in enumerate((
        (counts_hbm, counts_ref), (kernel_hbm, kernel_ref), (external_hbm, external_ref),
        (kin_hbm, kin_ref), (mag_hbm, mag_ref),
    ))]

    barrier = pltpu.get_barrier_semaphore()
    for k in range(1, devices):
        pl.semaphore_signal(barrier, inc=1, device_id=(partner(me, k),), device_id_type=pl.DeviceIdType.MESH)
    order = far_first(devices)

    def block(part, device, field=0):
        return pl.multiple_of(((part * devices + device) * local + field) * rows, 8)

    spread = max(rows_per // q_count, 1)
    x_row = lax.broadcasted_iota(jnp.int32, (nx, nx), 0)
    x_col = lax.broadcasted_iota(jnp.int32, (nx, nx), 1)
    x_row = x_of(x_row, devices, spread)

    def rolled(s, target, fields, field):
        picked = lax.rem(x_row - shift_ref[s] + nx, nx) == x_col
        pick = jnp.where(picked, 1.0, 0.0).astype(BF16)
        pick = jnp.concatenate([pick, pick], axis=1)
        slot_loads[s].wait()
        for h in range(cells // SLAB):
            high, low = halves(raw_ref[s, :, h * SLAB:(h + 1) * SLAB])
            moved = dot(pick, jnp.concatenate([high, low], axis=0))
            for k in range(SLAB // LANES):
                q = h * (SLAB // LANES) + k
                column = moved[:, k * LANES:(k + 1) * LANES]
                if rows_per >= q_count:
                    for xo in range(spread):
                        at = xo * q_count + q
                        start = (at // rows * devices * fields + field) * rows + at % rows
                        target[pl.ds(start, devices, stride=fields * rows), :] = (
                            column[xo * devices:(xo + 1) * devices]
                        )
                else:
                    start = (q // rows * fields + field) * rows + q % rows
                    target[pl.ds(start, nx, stride=q_count // rows * fields * rows), :] = column

    shift_load.wait()
    rolled(0, own_ref, local, 0)
    pl.semaphore_wait(barrier, devices - 1)

    sends = []
    arrivals = [[] for _ in range(parts)]

    def give(part, first, fields, k, send, recv):
        there = partner(me, k)
        copy = remote(own_ref.at[pl.ds(block(part, there, first), fields * rows)],
                      got_ref.at[pl.ds(block(part, me, first), fields * rows)], send.at[k], recv.at[k], there)
        copy.start()
        sends.append(copy)
        arrivals[part].append(copy)

    for k in order:
        give(0, 0, 1, k, lead_send, lead_recv)
    last = slot_each - 1
    rolled(last, out_ref, 1, 0)
    swap = remote(out_ref, in_ref, swap_sem.at[0], swap_sem.at[1], mate)
    swap.start()
    rolled(1, own_ref, local, 1)
    for copy in small:
        copy.wait()
    swap.wait_recv()
    lone = jnp.full((rows, LANES), counts_ref[me], jnp.int32) < local
    for part in range(parts):
        for dest in range(devices):
            where = ((part * devices + dest) * local + 1) * rows
            there = (part * devices + dest) * rows
            mine = own_ref[where:where + rows, :]
            own_ref[where:where + rows, :] = jnp.where(lone, in_ref[there:there + rows, :], mine)
    for k in order:
        give(0, 1, local - 1, k, part_send.at[0], part_recv.at[0])
    for part in range(1, parts):
        for k in order:
            give(part, 0, local, k, part_send.at[part], part_recv.at[part])
    for part in range(parts):
        got_ref[pl.ds(block(part, me), local * rows), :] = own_ref[pl.ds(block(part, me), local * rows), :]

    mixing_matrix(devices, counts_ref, kernel_ref, mix_ref)
    matrices(devices, kin_ref, mag_ref, xf_ref, xb_ref, kin_out, fwd_out, bwd_out)

    def mix(part):
        base = part * functions * rows
        for c in range(0, rows, 2):
            values = jnp.concatenate(
                [got_ref[pl.ds(base + c + k, functions, stride=rows), :] for k in range(2)], axis=1
            )
            high, low = halves(values)
            mixed = dot(mix_ref[...], jnp.concatenate([high, high, low], axis=0))
            up = down = 0.0
            for j in range(local):
                piece = mixed[j * devices:(j + 1) * devices]
                for k in range(2):
                    mixed_ref[pl.ds(base + j * rows + c + k, devices, stride=local * rows), :] = (
                        piece[:, k * LANES:(k + 1) * LANES]
                    )
                squared = piece * piece
                up = up + jnp.sum(squared[:half], axis=0, keepdims=True)
                down = down + jnp.sum(squared[half:], axis=0, keepdims=True)
            for k in range(2):
                up_ref[c + k:c + k + 1, :] = up[:, k * LANES:(k + 1) * LANES]
                down_ref[c + k:c + k + 1, :] = down[:, k * LANES:(k + 1) * LANES]
        rho_up, rho_down = up_ref[...] / count, down_ref[...] / count
        shared = external_ref[part * rows:(part + 1) * rows, :] + 0.5 * (rho_up + rho_down)
        spins = [shared - cube_root((6.0 / jnp.pi) * rho + 1e-6) for rho in (rho_up, rho_down)]
        for spin in range(2):
            pots_ref[spin, part * rows:(part + 1) * rows] = spins[spin]
        sizes = jnp.maximum(jnp.abs(spins[0]), jnp.abs(spins[1]))
        peak = sizes[:8]
        for w in range(1, rows // 8):
            peak = jnp.maximum(peak, sizes[w * 8:(w + 1) * 8])
        return peak

    peak = None
    returns, handed, waits = [], [], []
    for part in range(parts):
        for copy in arrivals[part]:
            copy.wait_recv()
        here = mix(part)
        peak = here if peak is None else jnp.maximum(peak, here)
        begin, extent = part * rows, rows
        if part == parts - 1:
            extent = rows + 8
            for spin in range(2):
                pots_ref[spin, rows_per:] = peak
        span = pl.ds(begin, extent)

        def show(source, owner, slot, there):
            copy = remote(source, gpot_ref.at[owner, span], pot_send.at[part, slot], pot_recv.at[part, slot], there)
            copy.start()
            return copy

        handed = show(pots_ref.at[1 - side, span], me, 0, across)
        sends.append(handed)
        for k in range(1, half):
            waits.append(show(pots_ref.at[side, span], me, k, partner(me, k)))
        for k in order:
            there = partner(me, k)
            copy = remote(mixed_ref.at[pl.ds(block(part, there), local * rows)],
                          back_ref.at[pl.ds(block(part, me), local * rows)],
                          back_send.at[part, k], back_recv.at[part, k], there)
            copy.start()
            returns.append(copy)
        back_ref[pl.ds(block(part, me), local * rows), :] = mixed_ref[pl.ds(block(part, me), local * rows), :]
        gpot_ref[me, begin:begin + extent] = pots_ref[side, begin:begin + extent]
        handed.wait_recv()
        for k in range(1, half):
            waits.append(show(gpot_ref.at[across, span], across, half + k, partner(me, k)))
    for copy in returns + waits:
        copy.wait_recv()
    for copy in [swap, *sends, *returns, *waits]:
        copy.wait_send()


def filter_kernel(devices, rows_per, parts, kin_ref, got_ref, gpot_ref, xf_ref, xb_ref, kinm_ref, fwd_ref, bwd_ref, out_ref,
                  v_hi, v_lo, p_hi, p_lo, w_hi, w_lo, acc_ref, pot_ref, stage_ref):
    local, nx, cells = out_ref.shape
    slabs = cells // SLAB
    q_count = cells // LANES
    per_slab = SLAB // LANES
    spread = max(rows_per // q_count, 1)

    rows = rows_per // parts
    pot_rows = gpot_ref.shape[0] // devices

    def plane(field, q):
        if field == local:
            ref, stride, extent = gpot_ref, pot_rows, rows_per
        else:
            ref, stride, extent = got_ref, local * rows, rows

        def start(x):
            if field == local:
                return x
            return (x // rows * devices * local + field) * rows + x % rows

        if rows_per >= q_count:
            return jnp.concatenate([
                ref[pl.ds(start(xo * q_count + q), devices, stride=stride), :] for xo in range(spread)
            ], axis=0)
        split = q_count // extent
        return ref[pl.ds((q // extent) * stride + start(q % extent), nx, stride=split * stride), :]

    def slab_of(field, h):
        return jnp.concatenate([plane(field, h * per_slab + k) for k in range(per_slab)], axis=1)

    for h in range(slabs):
        pot_ref[h] = slab_of(local, h)
        for f in range(local):
            high, low = halves(slab_of(f, h))
            where = slice(f * nx, (f + 1) * nx)
            v_hi[h, where] = high
            v_lo[h, where] = low
            both = dot(xf_ref[...], jnp.concatenate([high, high, low], axis=0))
            p_hi[h, where], p_lo[h, where] = halves(both[:nx])
            acc_ref[h, where] = both[nx:]

    def banded(hi_ref, lo_ref, matrix_ref, h):
        width = matrix_ref.shape[0] // 2
        count = width // SLAB

        def wide(ref):
            return jnp.concatenate([
                jnp.concatenate(
                    [ref[lax.rem(h + g + (n - count // 2) + slabs, slabs)] for n in range(count)], axis=1
                ) for g in range(GROUP)
            ], axis=0)

        high, low = wide(hi_ref), wide(lo_ref)
        return dot(high, matrix_ref[:width]) + (dot(low, matrix_ref[:width]) + dot(high, matrix_ref[width:]))

    def forward(step, carry):
        h = step * GROUP
        kinetic = banded(v_hi, v_lo, kinm_ref, h)
        smooth = banded(p_hi, p_lo, fwd_ref, h)
        for g in range(GROUP):
            base = g * local * nx
            acc_ref[h + g] += kinetic[base:base + local * nx]
            potential = pot_ref[h + g]
            for f in range(local):
                high, low = halves(smooth[base + f * nx:base + (f + 1) * nx] * potential)
                mixed = dot(xb_ref[...], jnp.concatenate([high, high, low], axis=0))
                w_hi[h + g, f * nx:(f + 1) * nx], w_lo[h + g, f * nx:(f + 1) * nx] = halves(mixed)
        return carry

    lax.fori_loop(0, slabs // GROUP, forward, 0)

    sides = jnp.abs(kin_ref[0])
    for t in range(1, kin_ref.shape[0]):
        sides = sides + 2.0 * jnp.abs(kin_ref[t])
    peaks = gpot_ref[rows_per:pot_rows, :]
    for e in range(1, devices):
        peaks = jnp.maximum(peaks, gpot_ref[e * pot_rows + rows_per:(e + 1) * pot_rows, :])
    bound = 1.0 + 1.5 * sides + jnp.max(peaks)

    def backward(step, carry):
        first = step * GROUP
        back = banded(w_hi, w_lo, bwd_ref, first)
        count = nx // spread
        for g in range(GROUP):
            h = first + g
            result = (acc_ref[h] + back[g * local * nx:(g + 1) * local * nx]) / bound
            for f in range(local):
                for k in range(per_slab):
                    q = h * per_slab + k
                    if spread > 1:
                        for xo in range(spread):
                            block = result[f * nx + xo * count:f * nx + (xo + 1) * count, k * LANES:(k + 1) * LANES]
                            stage_ref[f, q, pl.ds(xo, count, stride=spread), :] = block
                        ordered = stage_ref[f, q]
                    else:
                        ordered = result[f * nx:(f + 1) * nx, k * LANES:(k + 1) * LANES]
                    out_ref[f, :, pl.ds(pl.multiple_of(q * LANES, LANES), LANES)] = ordered
        return carry

    lax.fori_loop(0, slabs // GROUP, backward, 0)


def shaped(shape, dtype=F32):
    return jax.ShapeDtypeStruct(shape, dtype)


def body(support_functions, owner_counts, region_shift, kernel, external, kinetic_taps, magic_taps):
    devices = lax.axis_size("fn")
    slot_each, nx, cells = support_functions.shape
    functions = kernel.shape[0]
    local = functions // devices
    rows_per = nx * cells // devices // LANES
    q_count = cells // LANES
    parts = 2 if rows_per % (2 * q_count) == 0 else 1
    rows = rows_per // parts
    reach = -(-(magic_taps.shape[0] // 2) // YS)
    kin_reach = -(-(kinetic_taps.shape[0] - 1) // YS)

    each = pltpu.SemaphoreType.DMA((devices,))
    each_part = pltpu.SemaphoreType.DMA((parts, devices))
    flat = (nx * q_count, LANES)
    whole = (functions * rows_per, LANES)
    xf, xb, kin_m, fwd_m, bwd_m, back, gpot = pl.pallas_call(
        functools.partial(exchange_kernel, devices, parts),
        out_shape=(
            shaped((2 * nx, 3 * nx), BF16),
            shaped((nx, 3 * nx), BF16),
            shaped((2 * (2 * kin_reach + 1) * SLAB, SLAB), BF16),
            shaped((2 * (2 * reach + 1) * SLAB, SLAB), BF16),
            shaped((2 * (2 * reach + 1) * SLAB, SLAB), BF16),
            shaped(whole),
            shaped((devices, rows_per + 8, LANES)),
        ),
        in_specs=[HBM] * 7,
        out_specs=(VMEM,) * 7,
        scratch_shapes=[
            pltpu.VMEM((slot_each, nx, cells), F32), pltpu.VMEM(whole, F32),
            pltpu.VMEM(flat, F32), pltpu.VMEM(flat, F32), pltpu.VMEM(whole, F32), pltpu.VMEM(whole, F32),
            pltpu.VMEM((2, rows_per + 8, LANES), F32), pltpu.VMEM((functions, 3 * functions), BF16),
            pltpu.VMEM((functions, functions), F32), pltpu.VMEM((rows_per, LANES), F32),
            pltpu.VMEM((rows, LANES), F32), pltpu.VMEM((rows, LANES), F32),
            pltpu.SMEM(region_shift.shape, jnp.int32), pltpu.SMEM(owner_counts.shape, jnp.int32),
            pltpu.SMEM(kinetic_taps.shape, F32), pltpu.SMEM(magic_taps.shape, F32),
            pltpu.SemaphoreType.DMA((slot_each + 6,)), pltpu.SemaphoreType.DMA((2,)), each, each,
        ] + [each_part] * 6,
        compiler_params=params(collective_id=0),
        name="exchange",
    )(*(pltpu.with_memory_space_constraint(x, pltpu.HBM) for x in (
        support_functions, region_shift, owner_counts, kernel, external.reshape(rows_per, LANES),
        kinetic_taps, magic_taps,
    )))

    slabs = cells // SLAB
    tile = (slabs, local * nx, SLAB)
    return pl.pallas_call(
        functools.partial(filter_kernel, devices, rows_per, parts),
        out_shape=shaped((local, nx, cells)),
        in_specs=[SMEM] + [VMEM] * 7,
        out_specs=VMEM,
        scratch_shapes=[pltpu.VMEM(tile, BF16)] * 6
        + [pltpu.VMEM(tile, F32), pltpu.VMEM((slabs, nx, SLAB), F32),
           pltpu.VMEM((local, cells // LANES, nx, LANES), F32)],
        compiler_params=params(),
        name="filter",
    )(kinetic_taps, back, gpot.reshape(-1, LANES), xf, xb, kin_m, fwd_m, bwd_m)


def solution(mesh):
    placed = (P("fn", None, None), P(), P("fn"), P(), P("fn"), P(), P())
    return jax.shard_map(
        body, mesh=mesh, in_specs=placed, out_specs=P("fn", None, None), check_vma=False
    )
```

```python
import functools

import jax
import jax.numpy as jnp
from jax import lax
from jax.experimental import pallas as pl
from jax.experimental.pallas import tpu as pltpu
from jax.sharding import PartitionSpec as P

NY = 64
NZ = 32
LANES = 128
SLAB = 256
YS = SLAB // NZ
GROUP = 4
VMEM = pl.BlockSpec(memory_space=pltpu.VMEM)
SMEM = pl.BlockSpec(memory_space=pltpu.SMEM)
HBM = pl.BlockSpec(memory_space=pltpu.HBM)
F32 = jnp.float32
BF16 = jnp.bfloat16


def halves(values):
    high = values.astype(BF16)
    low = (values - high.astype(F32)).astype(BF16)
    return high, low


def dot(left, right):
    return jnp.dot(left, right, preferred_element_type=F32)


def params(**more):
    return pltpu.CompilerParams(vmem_limit_bytes=48 << 20, has_side_effects="collective_id" in more, **more)


def x_of(row, devices, spread):
    if spread == 1:
        return row
    return lax.rem(row, devices) * spread + row // devices


def matrices(devices, kin_ref, mag_ref, kx_out, kin_out, fwd_out, xf_ref, xb_ref, bwd_out):
    nx = xb_ref.shape[0]
    kin_half = kin_ref.shape[0]
    taps = mag_ref.shape[0]
    kin_count = 2 * kin_half - 1
    kin_center, mag_center = kin_count // 2, taps // 2
    kin = [-0.5 * kin_ref[abs(t - kin_center)] for t in range(kin_count)]
    mag = [mag_ref[t] for t in range(taps)]
    total = functools.reduce(lambda a, b: a + b, [jnp.abs(m) for m in mag])

    def picked(index, values, first=0):
        summed = jnp.zeros(index.shape, F32)
        for t, value in enumerate(values):
            summed = jnp.where(index == t + first, value, summed)
        return summed

    def iota(shape, dim):
        return lax.broadcasted_iota(jnp.int32, shape, dim)

    parts = kx_out.shape[0]
    plain = iota((nx, nx), 0)
    out_x, in_x = (x_of(iota((nx, nx), d), devices, parts) for d in (0, 1))
    ahead = lax.rem(in_x - out_x + mag_center + nx, nx)
    behind = lax.rem(plain - in_x + mag_center + nx, nx)
    across = lax.rem(in_x - plain + kin_center + nx, nx)
    fh, fl = halves(picked(ahead, mag) / total)
    kh, kl = halves(picked(across, kin))
    bh, bl = halves(picked(behind, mag) / total)
    xf_ref[...] = jnp.concatenate([fh, fl, fh], axis=1)
    xb_ref[...] = jnp.concatenate([bh, bl, bh], axis=1)
    each = nx // parts
    for part in range(parts):
        columns = slice(part * each, (part + 1) * each)
        kx_out[part] = jnp.concatenate([kh[:, columns], kl[:, columns], kh[:, columns]], axis=1)

    square = (SLAB, SLAB)
    row, col = iota(square, 0), iota(square, 1)
    in_y, in_z = row // NZ, lax.rem(row, NZ)
    out_y, out_z = col // NZ, lax.rem(col, NZ)
    dy, dz = in_y - out_y, in_z - out_z

    def along_y(delta, values, center, d):
        low = max(YS * d + center - (YS - 1), 0)
        high = min(YS * d + center + YS - 1, len(values) - 1)
        return picked(delta + (YS * d + center), values[low:high + 1], low)

    mag_z = picked(lax.rem(dz + mag_center + NZ, NZ), mag) / total
    mag_zt = picked(lax.rem(mag_center - dz + NZ, NZ), mag) / total
    kin_z = picked(lax.rem(dz + kin_center + NZ, NZ), kin)
    reach = fwd_out.shape[0] // 2 // SLAB // 2
    kin_reach = kin_out.shape[0] // 2 // SLAB // 2
    for n in range(2 * reach + 1):
        d = n - reach
        for out, y_part, z_part in (
            (fwd_out, along_y(dy, mag, mag_center, d), mag_z),
            (bwd_out, along_y(-dy, mag, mag_center, -d), mag_zt),
        ):
            high, low = halves(y_part / total * z_part)
            out[n * SLAB:(n + 1) * SLAB] = high
            base = (2 * reach + 1 + n) * SLAB
            out[base:base + SLAB] = low
    for n in range(2 * kin_reach + 1):
        d = n - kin_reach
        value = jnp.where(dz == 0, along_y(dy, kin, kin_center, d), 0.0)
        if d == 0:
            value = value + jnp.where(dy == 0, kin_z, 0.0)
        high, low = halves(value)
        kin_out[n * SLAB:(n + 1) * SLAB] = high
        base = (2 * kin_reach + 1 + n) * SLAB
        kin_out[base:base + SLAB] = low


def mixing_matrix(devices, counts_ref, kernel_ref, mix_out):
    functions = kernel_ref.shape[0]
    local = functions // devices
    full = (functions, functions)
    row, col = (lax.broadcasted_iota(jnp.int32, full, d) for d in (0, 1))
    lead = jnp.zeros((1, functions), jnp.int32)
    lane = lax.broadcasted_iota(jnp.int32, (1, functions), 1)
    pair = lane // (2 * local)
    for k in range(devices // 2):
        lead = jnp.where(pair == k, counts_ref[2 * k], lead)
    slot = lax.rem(lane, local)
    odd = lax.rem(lane // local, 2) == 1
    count = jnp.where(odd, 2 * local - lead, lead)
    first = jnp.where(odd, lead, 0)
    stand_in = jnp.where(odd, local, 2 * local - 1)
    second = jnp.where(count < local, stand_in, first + 1)
    place = pair * (2 * local) + jnp.where(slot == 0, first, second)
    wanted = lax.rem(row, devices) * local + row // devices
    row_pick = jnp.where(wanted == col, 1.0, 0.0).astype(BF16)
    col_pick = jnp.where(row == place, 1.0, 0.0).astype(BF16)
    parts = [dot(dot(row_pick, part).astype(BF16), col_pick).astype(BF16) for part in halves(kernel_ref[...])]
    mix_out[...] = jnp.concatenate([parts[0], parts[1], parts[0]], axis=1)


def partner(me, k):
    bit = 1
    there = me
    while bit <= k:
        if k & bit:
            there = there + bit - 2 * bit * ((me // bit) % 2)
        bit *= 2
    return there


def far_first(devices):
    half = devices // 2
    order = []
    for n in range(half):
        order += [half + n, n]
    return [k for k in order if k]


def remote(source, target, send, recv, device):
    return pltpu.make_async_remote_copy(
        src_ref=source, dst_ref=target, send_sem=send, recv_sem=recv,
        device_id=(device,), device_id_type=pl.DeviceIdType.MESH,
    )


def cube_root(x):
    guess = jnp.exp(jnp.log(x) * (1.0 / 3.0))
    return guess - (guess - x / (guess * guess)) * (1.0 / 3.0)


def banded(matrix_ref, high, low, slabs, wanted):
    width = matrix_ref.shape[0] // 2
    count = width // SLAB

    def wide(at):
        return jnp.concatenate([
            jnp.concatenate([at((h + n - count // 2) % slabs) for n in range(count)], axis=1) for h in wanted
        ], axis=0)

    high, low = wide(high), wide(low)
    return dot(high, matrix_ref[:width]) + (dot(low, matrix_ref[:width]) + dot(high, matrix_ref[width:]))


def exchange_kernel(devices, parts,
                    slots_hbm, shift_hbm, counts_hbm, kernel_hbm, external_hbm, kin_hbm, mag_hbm,
                    xf_ref, xb_ref, bwd_out, u_hi, u_lo, acc_ref, gpot_ref,
                    kx_ref, kin_out, fwd_out, v_hi, v_lo, back_ref, raw_ref, own_ref, out_ref, in_ref, got_ref, mixed_ref, pots_ref,
                    mix_ref, kernel_ref, external_ref, up_ref, down_ref,
                    shift_ref, counts_ref, kin_ref, mag_ref,
                    load_sem, swap_sem, lead_send, lead_recv, part_send, part_recv,
                    back_send, back_recv, pot_send, pot_recv):
    slot_each, nx, cells = raw_ref.shape
    functions = kernel_ref.shape[0]
    local = functions // devices
    q_count = cells // LANES
    rows_per = external_ref.shape[0]
    rows = rows_per // parts
    half = devices // 2
    count = functions // 2
    me = lax.axis_index("fn")
    side = me // half
    across = partner(me, half)
    mate = partner(me, 1)

    def load(source, target, k):
        copy = pltpu.make_async_copy(source, target, load_sem.at[k])
        copy.start()
        return copy

    slot_loads = {0: load(slots_hbm.at[0], raw_ref.at[0], 0)}
    shift_load = load(shift_hbm, shift_ref, slot_each)
    for s in reversed(range(1, slot_each)):
        slot_loads[s] = load(slots_hbm.at[s], raw_ref.at[s], s)
    small = [load(a, b, slot_each + 1 + k) for k, (a, b) in enumerate((
        (counts_hbm, counts_ref), (kernel_hbm, kernel_ref), (external_hbm, external_ref),
        (kin_hbm, kin_ref), (mag_hbm, mag_ref),
    ))]

    barrier = pltpu.get_barrier_semaphore()
    for k in range(1, devices):
        pl.semaphore_signal(barrier, inc=1, device_id=(partner(me, k),), device_id_type=pl.DeviceIdType.MESH)
    order = far_first(devices)

    def block(part, device, field=0):
        return pl.multiple_of(((part * devices + device) * local + field) * rows, 8)

    spread = max(rows_per // q_count, 1)
    x_row = lax.broadcasted_iota(jnp.int32, (nx, nx), 0)
    x_col = lax.broadcasted_iota(jnp.int32, (nx, nx), 1)
    x_row = x_of(x_row, devices, spread)

    def rolled(s, target, fields, field):
        picked = lax.rem(x_row - shift_ref[s] + nx, nx) == x_col
        pick = jnp.where(picked, 1.0, 0.0).astype(BF16)
        pick = jnp.concatenate([pick, pick], axis=1)
        slot_loads[s].wait()
        for h in range(cells // SLAB):
            high, low = halves(raw_ref[s, :, h * SLAB:(h + 1) * SLAB])
            moved = dot(pick, jnp.concatenate([high, low], axis=0))
            for k in range(SLAB // LANES):
                q = h * (SLAB // LANES) + k
                column = moved[:, k * LANES:(k + 1) * LANES]
                if rows_per >= q_count:
                    for xo in range(spread):
                        at = xo * q_count + q
                        start = (at // rows * devices * fields + field) * rows + at % rows
                        target[pl.ds(start, devices, stride=fields * rows), :] = (
                            column[xo * devices:(xo + 1) * devices]
                        )
                else:
                    start = (q // rows * fields + field) * rows + q % rows
                    target[pl.ds(start, nx, stride=q_count // rows * fields * rows), :] = column

    shift_load.wait()
    rolled(0, own_ref, local, 0)
    pl.semaphore_wait(barrier, devices - 1)

    sends = []
    arrivals = [[] for _ in range(parts)]

    def give(part, first, fields, k, send, recv):
        there = partner(me, k)
        copy = remote(own_ref.at[pl.ds(block(part, there, first), fields * rows)],
                      got_ref.at[pl.ds(block(part, me, first), fields * rows)], send.at[k], recv.at[k], there)
        copy.start()
        sends.append(copy)
        arrivals[part].append(copy)

    for k in order:
        give(0, 0, 1, k, lead_send, lead_recv)
    last = slot_each - 1
    rolled(last, out_ref, 1, 0)
    swap = remote(out_ref, in_ref, swap_sem.at[0], swap_sem.at[1], mate)
    swap.start()
    rolled(1, own_ref, local, 1)
    for copy in small:
        copy.wait()
    swap.wait_recv()
    lone = jnp.full((rows, LANES), counts_ref[me], jnp.int32) < local
    for part in range(parts):
        for dest in range(devices):
            where = ((part * devices + dest) * local + 1) * rows
            there = (part * devices + dest) * rows
            mine = own_ref[where:where + rows, :]
            own_ref[where:where + rows, :] = jnp.where(lone, in_ref[there:there + rows, :], mine)
    for k in order:
        give(0, 1, local - 1, k, part_send.at[0], part_recv.at[0])
    for part in range(1, parts):
        for k in order:
            give(part, 0, local, k, part_send.at[part], part_recv.at[part])
    for part in range(parts):
        got_ref[pl.ds(block(part, me), local * rows), :] = own_ref[pl.ds(block(part, me), local * rows), :]

    mixing_matrix(devices, counts_ref, kernel_ref, mix_ref)
    matrices(devices, kin_ref, mag_ref, kx_ref, kin_out, fwd_out, xf_ref, xb_ref, bwd_out)
    acc_ref[...] = jnp.zeros_like(acc_ref)
    slabs = cells // SLAB
    per_slab = SLAB // LANES
    each = nx // parts
    split = max(q_count // rows, 1)

    def forward(part, first, n):
        group = max(1, min(slabs, GROUP * each // n))
        length = n * split * local * rows
        begin = pl.multiple_of((part * devices + first * split) * local * rows, 8)
        view = back_ref.at[pl.ds(begin, length)]

        def where(f):
            return pl.ds(pl.multiple_of((part * local + f) * each + first, 16), n)

        for h in range(slabs):
            for f in range(local):
                value = jnp.concatenate([
                    view[pl.ds((q // rows * local + f) * rows + q % rows, n, stride=split * local * rows), :]
                    for q in range(h * per_slab, (h + 1) * per_slab)
                ], axis=1)
                v_hi[h, where(f)], v_lo[h, where(f)] = halves(value)

        def at(ref):
            return lambda h: jnp.concatenate([ref[h, where(f)] for f in range(local)], axis=0)

        for step in range(0, slabs, group):
            wanted = range(step, step + group)
            kinetic = banded(kin_out, at(v_hi), at(v_lo), slabs, wanted)
            smooth = banded(fwd_out, at(v_hi), at(v_lo), slabs, wanted)
            for g, h in enumerate(wanted):
                for f in range(local):
                    base = (g * local + f) * n
                    u_hi[h, where(f)], u_lo[h, where(f)] = halves(smooth[base:base + n])
                    rows_at = pl.ds(pl.multiple_of(f * nx + first * parts, 8), n * parts)
                    for k in range(per_slab):
                        target = acc_ref.at[h * per_slab + k, rows_at]
                        some = pl.ds(part, n, stride=parts) if parts > 1 else slice(None)
                        target[some, :] += kinetic[base:base + n, k * LANES:(k + 1) * LANES]

    def along_x(part):
        for h in range(slabs):
            for f in range(local):
                here = slice((part * local + f) * each, (part * local + f + 1) * each)
                high, low = v_hi[h, here], v_lo[h, here]
                moved = dot(kx_ref[part], jnp.concatenate([high, high, low], axis=0))
                for k in range(per_slab):
                    acc_ref[h * per_slab + k, f * nx:(f + 1) * nx, :] += moved[:, k * LANES:(k + 1) * LANES]

    def mix(part):
        base = part * functions * rows
        for c in range(0, rows, 2):
            values = jnp.concatenate(
                [got_ref[pl.ds(base + c + k, functions, stride=rows), :] for k in range(2)], axis=1
            )
            high, low = halves(values)
            mixed = dot(mix_ref[...], jnp.concatenate([high, high, low], axis=0))
            up = down = 0.0
            for j in range(local):
                piece = mixed[j * devices:(j + 1) * devices]
                for k in range(2):
                    mixed_ref[pl.ds(base + j * rows + c + k, devices, stride=local * rows), :] = (
                        piece[:, k * LANES:(k + 1) * LANES]
                    )
                squared = piece * piece
                up = up + jnp.sum(squared[:half], axis=0, keepdims=True)
                down = down + jnp.sum(squared[half:], axis=0, keepdims=True)
            for k in range(2):
                up_ref[c + k:c + k + 1, :] = up[:, k * LANES:(k + 1) * LANES]
                down_ref[c + k:c + k + 1, :] = down[:, k * LANES:(k + 1) * LANES]
        rho_up, rho_down = up_ref[...] / count, down_ref[...] / count
        shared = external_ref[part * rows:(part + 1) * rows, :] + 0.5 * (rho_up + rho_down)
        spins = [shared - cube_root((6.0 / jnp.pi) * rho + 1e-6) for rho in (rho_up, rho_down)]
        for spin in range(2):
            pots_ref[spin, part * rows:(part + 1) * rows] = spins[spin]
        sizes = jnp.maximum(jnp.abs(spins[0]), jnp.abs(spins[1]))
        peak = sizes[:8]
        for w in range(1, rows // 8):
            peak = jnp.maximum(peak, sizes[w * 8:(w + 1) * 8])
        return peak

    peak = None
    returns, waits = [[] for _ in range(parts)], []
    for part in range(parts):
        for copy in arrivals[part]:
            copy.wait_recv()
        here = mix(part)
        peak = here if peak is None else jnp.maximum(peak, here)
        begin, extent = part * rows, rows
        if part == parts - 1:
            extent = rows + 8
            for spin in range(2):
                pots_ref[spin, rows_per:] = peak
        span = pl.ds(begin, extent)

        def show(source, owner, slot, there):
            copy = remote(source, gpot_ref.at[owner, span], pot_send.at[part, slot], pot_recv.at[part, slot], there)
            copy.start()
            return copy

        handed = show(pots_ref.at[1 - side, span], me, 0, across)
        sends.append(handed)
        for k in range(1, half):
            waits.append(show(pots_ref.at[side, span], me, k, partner(me, k)))
        for k in order:
            there = partner(me, k)
            copy = remote(mixed_ref.at[pl.ds(block(part, there), local * rows)],
                          back_ref.at[pl.ds(block(part, me), local * rows)],
                          back_send.at[part, k], back_recv.at[part, k], there)
            copy.start()
            returns[part].append((k, copy))
        back_ref[pl.ds(block(part, me), local * rows), :] = mixed_ref[pl.ds(block(part, me), local * rows), :]
        gpot_ref[me, begin:begin + extent] = pots_ref[side, begin:begin + extent]
        handed.wait_recv()
        for k in range(1, half):
            waits.append(show(gpot_ref.at[across, span], across, half + k, partner(me, k)))

    for part in range(parts - 1):
        for _, copy in returns[part]:
            copy.wait_recv()
        forward(part, 0, each)
        along_x(part)
    final = parts - 1
    for near in (True, False):
        for k, copy in returns[final]:
            if (k < half) == near:
                copy.wait_recv()
        forward(final, (side if near else 1 - side) * (each // 2), each // 2)
    along_x(final)
    for copy in waits:
        copy.wait_recv()
    for copy in [swap, *sends, *waits, *(copy for part in returns for _, copy in part)]:
        copy.wait_send()


def filter_kernel(devices, rows_per, kin_ref, u_hi, u_lo, acc_ref, gpot_ref, xf_ref, xb_ref, bwd_ref, out_hbm,
                  w_hi, w_lo, out_ref, out_sem):
    local, nx, cells = out_ref.shape
    slabs = cells // SLAB
    q_count = cells // LANES
    per_slab = SLAB // LANES
    parts = max(rows_per // q_count, 1)
    each = nx // parts
    pot_rows = gpot_ref.shape[0] // devices

    def plane(q):
        if rows_per >= q_count:
            return jnp.concatenate([
                gpot_ref[pl.ds(xo * q_count + q, devices, stride=pot_rows), :] for xo in range(parts)
            ], axis=0)
        split = q_count // rows_per
        return gpot_ref[pl.ds((q // rows_per) * pot_rows + q % rows_per, nx, stride=split * pot_rows), :]

    sides = jnp.abs(kin_ref[0])
    for t in range(1, kin_ref.shape[0]):
        sides = sides + 2.0 * jnp.abs(kin_ref[t])
    peaks = gpot_ref[rows_per:pot_rows, :]
    for e in range(1, devices):
        peaks = jnp.maximum(peaks, gpot_ref[e * pot_rows + rows_per:(e + 1) * pot_rows, :])
    bound = 1.0 + 1.5 * sides + jnp.max(peaks)
    scale = 1.0 / jnp.full((1, SLAB), bound, F32)

    for h in range(slabs):
        potential = jnp.concatenate([plane(h * per_slab + k) for k in range(per_slab)], axis=1)
        for f in range(local):
            def taken(ref):
                starts = [(part * local + f) * each for part in range(parts)]
                return jnp.concatenate([ref[h, start:start + each] for start in starts], axis=0)

            high, low = taken(u_hi), taken(u_lo)
            smooth = dot(xf_ref[...], jnp.concatenate([high, high, low], axis=0))
            high, low = halves(smooth * potential)
            moved = dot(xb_ref[...], jnp.concatenate([high, high, low], axis=0))
            w_hi[h, f * nx:(f + 1) * nx], w_lo[h, f * nx:(f + 1) * nx] = halves(moved)

    copies = []
    for step in range(0, slabs, GROUP):
        wanted = range(step, step + GROUP)
        back = banded(bwd_ref, lambda h: w_hi[h], lambda h: w_lo[h], slabs, wanted)
        for g, h in enumerate(wanted):
            kinetic = jnp.concatenate([acc_ref[h * per_slab + k] for k in range(per_slab)], axis=1)
            result = (kinetic + back[g * local * nx:(g + 1) * local * nx]) * scale
            for f in range(local):
                out_ref[f, :, h * SLAB:(h + 1) * SLAB] = result[f * nx:(f + 1) * nx]
        columns = pl.ds(step * SLAB, GROUP * SLAB)
        copy = pltpu.make_async_copy(out_ref.at[:, :, columns], out_hbm.at[:, :, columns], out_sem.at[len(copies)])
        copy.start()
        copies.append(copy)
    for copy in copies:
        copy.wait()


def shaped(shape, dtype=F32):
    return jax.ShapeDtypeStruct(shape, dtype)


def body(support_functions, owner_counts, region_shift, kernel, external, kinetic_taps, magic_taps):
    devices = lax.axis_size("fn")
    slot_each, nx, cells = support_functions.shape
    functions = kernel.shape[0]
    local = functions // devices
    rows_per = nx * cells // devices // LANES
    q_count = cells // LANES
    parts = max(rows_per // q_count, 1)
    rows = rows_per // parts
    reach = -(-(magic_taps.shape[0] // 2) // YS)
    kin_reach = -(-(kinetic_taps.shape[0] - 1) // YS)

    each = pltpu.SemaphoreType.DMA((devices,))
    each_part = pltpu.SemaphoreType.DMA((parts, devices))
    flat = (nx * q_count, LANES)
    whole = (functions * rows_per, LANES)
    slabs = cells // SLAB
    tile = (slabs, local * nx, SLAB)
    kin_band = pltpu.VMEM((2 * (2 * kin_reach + 1) * SLAB, SLAB), BF16)
    mag_band = (2 * (2 * reach + 1) * SLAB, SLAB)
    xf, xb, bwd_m, u_hi, u_lo, acc, gpot = pl.pallas_call(
        functools.partial(exchange_kernel, devices, parts),
        out_shape=(
            shaped((nx, 3 * nx), BF16),
            shaped((nx, 3 * nx), BF16),
            shaped(mag_band, BF16),
            shaped(tile, BF16),
            shaped(tile, BF16),
            shaped((q_count, local * nx, LANES)),
            shaped((devices, rows_per + 8, LANES)),
        ),
        in_specs=[HBM] * 7,
        out_specs=(VMEM,) * 7,
        scratch_shapes=[
            pltpu.VMEM((parts, nx, 3 * nx // parts), BF16), kin_band, pltpu.VMEM(mag_band, BF16),
            pltpu.VMEM(tile, BF16), pltpu.VMEM(tile, BF16), pltpu.VMEM(whole, F32),
            pltpu.VMEM((slot_each, nx, cells), F32), pltpu.VMEM(whole, F32),
            pltpu.VMEM(flat, F32), pltpu.VMEM(flat, F32), pltpu.VMEM(whole, F32), pltpu.VMEM(whole, F32),
            pltpu.VMEM((2, rows_per + 8, LANES), F32), pltpu.VMEM((functions, 3 * functions), BF16),
            pltpu.VMEM((functions, functions), F32), pltpu.VMEM((rows_per, LANES), F32),
            pltpu.VMEM((rows, LANES), F32), pltpu.VMEM((rows, LANES), F32),
            pltpu.SMEM(region_shift.shape, jnp.int32), pltpu.SMEM(owner_counts.shape, jnp.int32),
            pltpu.SMEM(kinetic_taps.shape, F32), pltpu.SMEM(magic_taps.shape, F32),
            pltpu.SemaphoreType.DMA((slot_each + 6,)), pltpu.SemaphoreType.DMA((2,)), each, each,
        ] + [each_part] * 6,
        compiler_params=params(collective_id=0),
        name="exchange",
    )(*(pltpu.with_memory_space_constraint(x, pltpu.HBM) for x in (
        support_functions, region_shift, owner_counts, kernel, external.reshape(rows_per, LANES),
        kinetic_taps, magic_taps,
    )))

    return pl.pallas_call(
        functools.partial(filter_kernel, devices, rows_per),
        out_shape=shaped((local, nx, cells)),
        in_specs=[SMEM] + [VMEM] * 7,
        out_specs=HBM,
        scratch_shapes=[
            pltpu.VMEM(tile, BF16), pltpu.VMEM(tile, BF16), pltpu.VMEM((local, nx, cells), F32),
            pltpu.SemaphoreType.DMA((slabs // GROUP,)),
        ],
        compiler_params=params(),
        name="filter",
    )(kinetic_taps, u_hi, u_lo, acc, gpot.reshape(-1, LANES), xf, xb, bwd_m)


def solution(mesh):
    placed = (P("fn", None, None), P(), P("fn"), P(), P("fn"), P(), P())
    return jax.shard_map(
        body, mesh=mesh, in_specs=placed, out_specs=P("fn", None, None), check_vma=False
    )
```

```python
import functools

import jax
import jax.numpy as jnp
from jax import lax
from jax.experimental import pallas as pl
from jax.experimental.pallas import tpu as pltpu
from jax.sharding import PartitionSpec as P

NY = 64
NZ = 32
LANES = 128
SLAB = 256
YS = SLAB // NZ
GROUP = 4
VMEM = pl.BlockSpec(memory_space=pltpu.VMEM)
HBM = pl.BlockSpec(memory_space=pltpu.HBM)
F32 = jnp.float32
BF16 = jnp.bfloat16


def halves(values):
    high = values.astype(BF16)
    low = (values - high.astype(F32)).astype(BF16)
    return high, low


def dot(left, right):
    return jnp.dot(left, right, preferred_element_type=F32)


def params(**more):
    return pltpu.CompilerParams(vmem_limit_bytes=48 << 20, has_side_effects="collective_id" in more, **more)


def x_of(row, devices, spread):
    if spread == 1:
        return row
    return lax.rem(row, devices) * spread + row // devices


def matrices(devices, kin_ref, mag_ref, kx_out, kin_out, fwd_out, xf_ref, xb_ref, bwd_out):
    nx = xb_ref.shape[0]
    kin_half = kin_ref.shape[0]
    taps = mag_ref.shape[0]
    kin_count = 2 * kin_half - 1
    kin_center, mag_center = kin_count // 2, taps // 2
    kin = [-0.5 * kin_ref[abs(t - kin_center)] for t in range(kin_count)]
    mag = [mag_ref[t] for t in range(taps)]
    total = functools.reduce(lambda a, b: a + b, [jnp.abs(m) for m in mag])

    def picked(index, values, first=0):
        summed = jnp.zeros(index.shape, F32)
        for t, value in enumerate(values):
            summed = jnp.where(index == t + first, value, summed)
        return summed

    def iota(shape, dim):
        return lax.broadcasted_iota(jnp.int32, shape, dim)

    parts = kx_out.shape[0]
    plain = iota((nx, nx), 0)
    out_x, in_x = (x_of(iota((nx, nx), d), devices, parts) for d in (0, 1))
    ahead = lax.rem(in_x - out_x + mag_center + nx, nx)
    behind = lax.rem(plain - in_x + mag_center + nx, nx)
    across = lax.rem(in_x - plain + kin_center + nx, nx)
    fh, fl = halves(picked(ahead, mag) / total)
    kh, kl = halves(picked(across, kin))
    bh, bl = halves(picked(behind, mag) / total)
    xf_ref[...] = jnp.concatenate([fh, fl, fh], axis=1)
    xb_ref[...] = jnp.concatenate([bh, bl, bh], axis=1)
    each = nx // parts
    for part in range(parts):
        columns = slice(part * each, (part + 1) * each)
        kx_out[part] = jnp.concatenate([kh[:, columns], kl[:, columns], kh[:, columns]], axis=1)

    square = (SLAB, SLAB)
    row, col = iota(square, 0), iota(square, 1)
    in_y, in_z = row // NZ, lax.rem(row, NZ)
    out_y, out_z = col // NZ, lax.rem(col, NZ)
    dy, dz = in_y - out_y, in_z - out_z

    def along_y(delta, values, center, d):
        low = max(YS * d + center - (YS - 1), 0)
        high = min(YS * d + center + YS - 1, len(values) - 1)
        return picked(delta + (YS * d + center), values[low:high + 1], low)

    mag_z = picked(lax.rem(dz + mag_center + NZ, NZ), mag) / total
    mag_zt = picked(lax.rem(mag_center - dz + NZ, NZ), mag) / total
    kin_z = picked(lax.rem(dz + kin_center + NZ, NZ), kin)
    reach = fwd_out.shape[0] // 2 // SLAB // 2
    kin_reach = kin_out.shape[0] // 2 // SLAB // 2
    for n in range(2 * reach + 1):
        d = n - reach
        for out, y_part, z_part in (
            (fwd_out, along_y(dy, mag, mag_center, d), mag_z),
            (bwd_out, along_y(-dy, mag, mag_center, -d), mag_zt),
        ):
            high, low = halves(y_part / total * z_part)
            out[n * SLAB:(n + 1) * SLAB] = high
            base = (2 * reach + 1 + n) * SLAB
            out[base:base + SLAB] = low
    for n in range(2 * kin_reach + 1):
        d = n - kin_reach
        value = jnp.where(dz == 0, along_y(dy, kin, kin_center, d), 0.0)
        if d == 0:
            value = value + jnp.where(dy == 0, kin_z, 0.0)
        high, low = halves(value)
        kin_out[n * SLAB:(n + 1) * SLAB] = high
        base = (2 * kin_reach + 1 + n) * SLAB
        kin_out[base:base + SLAB] = low


def mixing_matrix(devices, counts_ref, kernel_ref, mix_out):
    functions = kernel_ref.shape[0]
    local = functions // devices
    full = (functions, functions)
    row, col = (lax.broadcasted_iota(jnp.int32, full, d) for d in (0, 1))
    lead = jnp.zeros((1, functions), jnp.int32)
    lane = lax.broadcasted_iota(jnp.int32, (1, functions), 1)
    pair = lane // (2 * local)
    for k in range(devices // 2):
        lead = jnp.where(pair == k, counts_ref[2 * k], lead)
    slot = lax.rem(lane, local)
    odd = lax.rem(lane // local, 2) == 1
    count = jnp.where(odd, 2 * local - lead, lead)
    first = jnp.where(odd, lead, 0)
    stand_in = jnp.where(odd, local, 2 * local - 1)
    second = jnp.where(count < local, stand_in, first + 1)
    place = pair * (2 * local) + jnp.where(slot == 0, first, second)
    wanted = lax.rem(row, devices) * local + row // devices
    row_pick = jnp.where(wanted == col, 1.0, 0.0).astype(BF16)
    col_pick = jnp.where(row == place, 1.0, 0.0).astype(BF16)
    parts = [dot(dot(row_pick, part).astype(BF16), col_pick).astype(BF16) for part in halves(kernel_ref[...])]
    mix_out[...] = jnp.concatenate([parts[0], parts[1], parts[0]], axis=1)


def partner(me, k):
    bit = 1
    there = me
    while bit <= k:
        if k & bit:
            there = there + bit - 2 * bit * ((me // bit) % 2)
        bit *= 2
    return there


def far_first(devices):
    half = devices // 2
    order = []
    for n in range(half):
        order += [half + n, n]
    return [k for k in order if k]


def remote(source, target, send, recv, device):
    return pltpu.make_async_remote_copy(
        src_ref=source, dst_ref=target, send_sem=send, recv_sem=recv,
        device_id=(device,), device_id_type=pl.DeviceIdType.MESH,
    )


def cube_root(x):
    guess = jnp.exp(jnp.log(x) * (1.0 / 3.0))
    return guess - (guess - x / (guess * guess)) * (1.0 / 3.0)


def banded(matrix_ref, high, low, slabs, wanted):
    width = matrix_ref.shape[0] // 2
    count = width // SLAB

    def wide(at):
        return jnp.concatenate([
            jnp.concatenate([at((h + n - count // 2) % slabs) for n in range(count)], axis=1) for h in wanted
        ], axis=0)

    high, low = wide(high), wide(low)
    return dot(high, matrix_ref[:width]) + (dot(low, matrix_ref[:width]) + dot(high, matrix_ref[width:]))


def exchange_kernel(devices, parts,
                    slots_hbm, shift_hbm, counts_hbm, kernel_hbm, external_hbm, kin_hbm, mag_hbm,
                    xf_ref, xb_ref, bwd_out, u_hi, u_lo, acc_ref, sides_ref, gpot_ref,
                    kx_ref, kin_out, fwd_out, v_hi, v_lo, back_ref, raw_ref, own_ref, out_ref, in_ref, got_ref, mixed_ref, pots_ref,
                    mix_ref, kernel_ref, external_ref, up_ref, down_ref,
                    shift_ref, counts_ref, kin_ref, mag_ref,
                    load_sem, swap_sem, lead_send, lead_recv, part_send, part_recv,
                    back_send, back_recv, pot_send, pot_recv):
    slot_each, nx, cells = raw_ref.shape
    functions = kernel_ref.shape[0]
    local = functions // devices
    q_count = cells // LANES
    rows_per = external_ref.shape[0]
    rows = rows_per // parts
    half = devices // 2
    count = functions // 2
    me = lax.axis_index("fn")
    side = me // half
    across = partner(me, half)
    mate = partner(me, 1)

    def load(source, target, k):
        copy = pltpu.make_async_copy(source, target, load_sem.at[k])
        copy.start()
        return copy

    slot_loads = {0: load(slots_hbm.at[0], raw_ref.at[0], 0)}
    shift_load = load(shift_hbm, shift_ref, slot_each)
    for s in reversed(range(1, slot_each)):
        slot_loads[s] = load(slots_hbm.at[s], raw_ref.at[s], s)
    small = [load(a, b, slot_each + 1 + k) for k, (a, b) in enumerate((
        (counts_hbm, counts_ref), (kernel_hbm, kernel_ref), (external_hbm, external_ref),
        (kin_hbm, kin_ref), (mag_hbm, mag_ref),
    ))]

    barrier = pltpu.get_barrier_semaphore()
    for k in range(1, devices):
        pl.semaphore_signal(barrier, inc=1, device_id=(partner(me, k),), device_id_type=pl.DeviceIdType.MESH)
    order = far_first(devices)

    def block(part, device, field=0):
        return pl.multiple_of(((part * devices + device) * local + field) * rows, 8)

    spread = max(rows_per // q_count, 1)
    x_row = lax.broadcasted_iota(jnp.int32, (nx, nx), 0)
    x_col = lax.broadcasted_iota(jnp.int32, (nx, nx), 1)
    x_row = x_of(x_row, devices, spread)

    def rolled(s, target, fields, field):
        picked = lax.rem(x_row - shift_ref[s] + nx, nx) == x_col
        pick = jnp.where(picked, 1.0, 0.0).astype(BF16)
        pick = jnp.concatenate([pick, pick], axis=1)
        slot_loads[s].wait()
        for h in range(cells // SLAB):
            high, low = halves(raw_ref[s, :, h * SLAB:(h + 1) * SLAB])
            moved = dot(pick, jnp.concatenate([high, low], axis=0))
            for k in range(SLAB // LANES):
                q = h * (SLAB // LANES) + k
                column = moved[:, k * LANES:(k + 1) * LANES]
                if rows_per >= q_count:
                    for xo in range(spread):
                        at = xo * q_count + q
                        start = (at // rows * devices * fields + field) * rows + at % rows
                        target[pl.ds(start, devices, stride=fields * rows), :] = (
                            column[xo * devices:(xo + 1) * devices]
                        )
                else:
                    start = (q // rows * fields + field) * rows + q % rows
                    target[pl.ds(start, nx, stride=q_count // rows * fields * rows), :] = column

    shift_load.wait()
    rolled(0, own_ref, local, 0)
    pl.semaphore_wait(barrier, devices - 1)

    sends = []
    arrivals = [[] for _ in range(parts)]

    def give(part, first, fields, k, send, recv):
        there = partner(me, k)
        copy = remote(own_ref.at[pl.ds(block(part, there, first), fields * rows)],
                      got_ref.at[pl.ds(block(part, me, first), fields * rows)], send.at[k], recv.at[k], there)
        copy.start()
        sends.append(copy)
        arrivals[part].append(copy)

    for k in order:
        give(0, 0, 1, k, lead_send, lead_recv)
    last = slot_each - 1
    rolled(last, out_ref, 1, 0)
    swap = remote(out_ref, in_ref, swap_sem.at[0], swap_sem.at[1], mate)
    swap.start()
    rolled(1, own_ref, local, 1)
    for copy in small:
        copy.wait()
    swap.wait_recv()
    lone = jnp.full((rows, LANES), counts_ref[me], jnp.int32) < local
    for part in range(parts):
        for dest in range(devices):
            where = ((part * devices + dest) * local + 1) * rows
            there = (part * devices + dest) * rows
            mine = own_ref[where:where + rows, :]
            own_ref[where:where + rows, :] = jnp.where(lone, in_ref[there:there + rows, :], mine)
    for k in order:
        give(0, 1, local - 1, k, part_send.at[0], part_recv.at[0])
    for part in range(1, parts):
        for k in order:
            give(part, 0, local, k, part_send.at[part], part_recv.at[part])
    for part in range(parts):
        got_ref[pl.ds(block(part, me), local * rows), :] = own_ref[pl.ds(block(part, me), local * rows), :]

    mixing_matrix(devices, counts_ref, kernel_ref, mix_ref)
    matrices(devices, kin_ref, mag_ref, kx_ref, kin_out, fwd_out, xf_ref, xb_ref, bwd_out)
    acc_ref[...] = jnp.zeros_like(acc_ref)
    sides = jnp.abs(kin_ref[0])
    for t in range(1, kin_ref.shape[0]):
        sides = sides + 2.0 * jnp.abs(kin_ref[t])
    sides_ref[...] = jnp.full(sides_ref.shape, 1.0 + 1.5 * sides, F32)
    slabs = cells // SLAB
    per_slab = SLAB // LANES
    each = nx // parts
    split = max(q_count // rows, 1)

    def forward(part, first, n):
        group = GROUP
        length = n * split * local * rows
        begin = pl.multiple_of((part * devices + first * split) * local * rows, 8)
        view = back_ref.at[pl.ds(begin, length)]

        def where(f):
            return pl.ds(pl.multiple_of((part * local + f) * each + first, 16), n)

        for h in range(slabs):
            for f in range(local):
                value = jnp.concatenate([
                    view[pl.ds((q // rows * local + f) * rows + q % rows, n, stride=split * local * rows), :]
                    for q in range(h * per_slab, (h + 1) * per_slab)
                ], axis=1)
                v_hi[h, where(f)], v_lo[h, where(f)] = halves(value)

        def at(ref):
            return lambda h: jnp.concatenate([ref[h, where(f)] for f in range(local)], axis=0)

        for step in range(0, slabs, group):
            wanted = range(step, step + group)
            kinetic = banded(kin_out, at(v_hi), at(v_lo), slabs, wanted)
            smooth = banded(fwd_out, at(v_hi), at(v_lo), slabs, wanted)
            for g, h in enumerate(wanted):
                for f in range(local):
                    base = (g * local + f) * n
                    u_hi[h, where(f)], u_lo[h, where(f)] = halves(smooth[base:base + n])
                    rows_at = pl.ds(pl.multiple_of(f * nx + first * parts, 8), n * parts)
                    for k in range(per_slab):
                        target = acc_ref.at[h * per_slab + k, rows_at]
                        some = pl.ds(part, n, stride=parts) if parts > 1 else slice(None)
                        target[some, :] += kinetic[base:base + n, k * LANES:(k + 1) * LANES]

    def along_x(part):
        for h in range(slabs):
            for f in range(local):
                here = slice((part * local + f) * each, (part * local + f + 1) * each)
                high, low = v_hi[h, here], v_lo[h, here]
                moved = dot(kx_ref[part], jnp.concatenate([high, high, low], axis=0))
                for k in range(per_slab):
                    acc_ref[h * per_slab + k, f * nx:(f + 1) * nx, :] += moved[:, k * LANES:(k + 1) * LANES]

    def mix(part):
        base = part * functions * rows
        for c in range(0, rows, 2):
            values = jnp.concatenate(
                [got_ref[pl.ds(base + c + k, functions, stride=rows), :] for k in range(2)], axis=1
            )
            high, low = halves(values)
            mixed = dot(mix_ref[...], jnp.concatenate([high, high, low], axis=0))
            up = down = 0.0
            for j in range(local):
                piece = mixed[j * devices:(j + 1) * devices]
                for k in range(2):
                    mixed_ref[pl.ds(base + j * rows + c + k, devices, stride=local * rows), :] = (
                        piece[:, k * LANES:(k + 1) * LANES]
                    )
                squared = piece * piece
                up = up + jnp.sum(squared[:half], axis=0, keepdims=True)
                down = down + jnp.sum(squared[half:], axis=0, keepdims=True)
            for k in range(2):
                up_ref[c + k:c + k + 1, :] = up[:, k * LANES:(k + 1) * LANES]
                down_ref[c + k:c + k + 1, :] = down[:, k * LANES:(k + 1) * LANES]
        rho_up, rho_down = up_ref[...] / count, down_ref[...] / count
        shared = external_ref[part * rows:(part + 1) * rows, :] + 0.5 * (rho_up + rho_down)
        spins = [shared - cube_root((6.0 / jnp.pi) * rho + 1e-6) for rho in (rho_up, rho_down)]
        for spin in range(2):
            pots_ref[spin, part * rows:(part + 1) * rows] = spins[spin]
        sizes = jnp.maximum(jnp.abs(spins[0]), jnp.abs(spins[1]))
        peak = sizes[:8]
        for w in range(1, rows // 8):
            peak = jnp.maximum(peak, sizes[w * 8:(w + 1) * 8])
        return peak

    peak = None
    returns, waits = [[] for _ in range(parts)], []
    for part in range(parts):
        for copy in arrivals[part]:
            copy.wait_recv()
        here = mix(part)
        peak = here if peak is None else jnp.maximum(peak, here)
        begin, extent = part * rows, rows
        if part == parts - 1:
            extent = rows + 1
            for spin in range(2):
                pots_ref[spin, rows_per:rows_per + 1] = jnp.max(peak, axis=0, keepdims=True)
        span = pl.ds(begin, extent)

        def show(source, owner, slot, there):
            copy = remote(source, gpot_ref.at[owner, span], pot_send.at[part, slot], pot_recv.at[part, slot], there)
            copy.start()
            return copy

        handed = show(pots_ref.at[1 - side, span], me, 0, across)
        sends.append(handed)
        for k in range(1, half):
            waits.append(show(pots_ref.at[side, span], me, k, partner(me, k)))
        for k in order:
            there = partner(me, k)
            copy = remote(mixed_ref.at[pl.ds(block(part, there), local * rows)],
                          back_ref.at[pl.ds(block(part, me), local * rows)],
                          back_send.at[part, k], back_recv.at[part, k], there)
            copy.start()
            returns[part].append((k, copy))
        back_ref[pl.ds(block(part, me), local * rows), :] = mixed_ref[pl.ds(block(part, me), local * rows), :]
        gpot_ref[me, begin:begin + extent] = pots_ref[side, begin:begin + extent]
        handed.wait_recv()
        for k in range(1, half):
            waits.append(show(gpot_ref.at[across, span], across, half + k, partner(me, k)))

    for part in range(parts - 1):
        for _, copy in returns[part]:
            copy.wait_recv()
        forward(part, 0, each)
        along_x(part)
    final = parts - 1
    for near in (True, False):
        for k, copy in returns[final]:
            if (k < half) == near:
                copy.wait_recv()
        forward(final, (side if near else 1 - side) * (each // 2), each // 2)
    along_x(final)
    for copy in waits:
        copy.wait_recv()
    for copy in [swap, *sends, *waits, *(copy for part in returns for _, copy in part)]:
        copy.wait_send()


def filter_kernel(devices, rows_per, u_hi, u_lo, acc_ref, sides_ref, gpot_ref, xf_ref, xb_ref, bwd_ref, out_hbm,
                  w_hi, w_lo, out_ref, out_sem):
    local, nx, cells = out_ref.shape
    slabs = cells // SLAB
    q_count = cells // LANES
    per_slab = SLAB // LANES
    parts = max(rows_per // q_count, 1)
    each = nx // parts
    pot_rows = gpot_ref.shape[0] // devices

    def plane(q):
        if rows_per >= q_count:
            return jnp.concatenate([
                gpot_ref[pl.ds(xo * q_count + q, devices, stride=pot_rows), :] for xo in range(parts)
            ], axis=0)
        split = q_count // rows_per
        return gpot_ref[pl.ds((q // rows_per) * pot_rows + q % rows_per, nx, stride=split * pot_rows), :]

    peaks = gpot_ref[pl.ds(rows_per, devices, stride=pot_rows), :]
    bound = sides_ref[:1, :] + jnp.max(peaks)
    scale = jnp.concatenate([1.0 / bound] * per_slab, axis=1)

    for h in range(slabs):
        potential = jnp.concatenate([plane(h * per_slab + k) for k in range(per_slab)], axis=1)
        for f in range(local):
            def taken(ref):
                starts = [(part * local + f) * each for part in range(parts)]
                return jnp.concatenate([ref[h, start:start + each] for start in starts], axis=0)

            high, low = taken(u_hi), taken(u_lo)
            smooth = dot(xf_ref[...], jnp.concatenate([high, high, low], axis=0))
            high, low = halves(smooth * potential)
            moved = dot(xb_ref[...], jnp.concatenate([high, high, low], axis=0))
            w_hi[h, f * nx:(f + 1) * nx], w_lo[h, f * nx:(f + 1) * nx] = halves(moved)

    copies = []
    group = slabs // out_sem.shape[0]
    for step in range(0, slabs, group):
        wanted = range(step, step + group)
        back = banded(bwd_ref, lambda h: w_hi[h], lambda h: w_lo[h], slabs, wanted)
        for g, h in enumerate(wanted):
            kinetic = jnp.concatenate([acc_ref[h * per_slab + k] for k in range(per_slab)], axis=1)
            result = (kinetic + back[g * local * nx:(g + 1) * local * nx]) * scale
            for f in range(local):
                out_ref[f, :, h * SLAB:(h + 1) * SLAB] = result[f * nx:(f + 1) * nx]
        columns = pl.ds(step * SLAB, group * SLAB)
        copy = pltpu.make_async_copy(out_ref.at[:, :, columns], out_hbm.at[:, :, columns], out_sem.at[len(copies)])
        copy.start()
        copies.append(copy)
    for copy in copies:
        copy.wait()


def shaped(shape, dtype=F32):
    return jax.ShapeDtypeStruct(shape, dtype)


def body(support_functions, owner_counts, region_shift, kernel, external, kinetic_taps, magic_taps):
    devices = lax.axis_size("fn")
    slot_each, nx, cells = support_functions.shape
    functions = kernel.shape[0]
    local = functions // devices
    rows_per = nx * cells // devices // LANES
    q_count = cells // LANES
    parts = max(rows_per // q_count, 1)
    rows = rows_per // parts
    reach = -(-(magic_taps.shape[0] // 2) // YS)
    kin_reach = -(-(kinetic_taps.shape[0] - 1) // YS)

    each = pltpu.SemaphoreType.DMA((devices,))
    each_part = pltpu.SemaphoreType.DMA((parts, devices))
    flat = (nx * q_count, LANES)
    whole = (functions * rows_per, LANES)
    slabs = cells // SLAB
    tile = (slabs, local * nx, SLAB)
    kin_band = pltpu.VMEM((2 * (2 * kin_reach + 1) * SLAB, SLAB), BF16)
    mag_band = (2 * (2 * reach + 1) * SLAB, SLAB)
    xf, xb, bwd_m, u_hi, u_lo, acc, sides, gpot = pl.pallas_call(
        functools.partial(exchange_kernel, devices, parts),
        out_shape=(
            shaped((nx, 3 * nx), BF16),
            shaped((nx, 3 * nx), BF16),
            shaped(mag_band, BF16),
            shaped(tile, BF16),
            shaped(tile, BF16),
            shaped((q_count, local * nx, LANES)),
            shaped((8, LANES)),
            shaped((devices, rows_per + 8, LANES)),
        ),
        in_specs=[HBM] * 7,
        out_specs=(VMEM,) * 8,
        scratch_shapes=[
            pltpu.VMEM((parts, nx, 3 * nx // parts), BF16), kin_band, pltpu.VMEM(mag_band, BF16),
            pltpu.VMEM(tile, BF16), pltpu.VMEM(tile, BF16), pltpu.VMEM(whole, F32),
            pltpu.VMEM((slot_each, nx, cells), F32), pltpu.VMEM(whole, F32),
            pltpu.VMEM(flat, F32), pltpu.VMEM(flat, F32), pltpu.VMEM(whole, F32), pltpu.VMEM(whole, F32),
            pltpu.VMEM((2, rows_per + 8, LANES), F32), pltpu.VMEM((functions, 3 * functions), BF16),
            pltpu.VMEM((functions, functions), F32), pltpu.VMEM((rows_per, LANES), F32),
            pltpu.VMEM((rows, LANES), F32), pltpu.VMEM((rows, LANES), F32),
            pltpu.SMEM(region_shift.shape, jnp.int32), pltpu.SMEM(owner_counts.shape, jnp.int32),
            pltpu.SMEM(kinetic_taps.shape, F32), pltpu.SMEM(magic_taps.shape, F32),
            pltpu.SemaphoreType.DMA((slot_each + 6,)), pltpu.SemaphoreType.DMA((2,)), each, each,
        ] + [each_part] * 6,
        compiler_params=params(collective_id=0),
        name="exchange",
    )(*(pltpu.with_memory_space_constraint(x, pltpu.HBM) for x in (
        support_functions, region_shift, owner_counts, kernel, external.reshape(rows_per, LANES),
        kinetic_taps, magic_taps,
    )))

    return pl.pallas_call(
        functools.partial(filter_kernel, devices, rows_per),
        out_shape=shaped((local, nx, cells)),
        in_specs=[VMEM] * 8,
        out_specs=HBM,
        scratch_shapes=[
            pltpu.VMEM(tile, BF16), pltpu.VMEM(tile, BF16), pltpu.VMEM((local, nx, cells), F32),
            pltpu.SemaphoreType.DMA((4,)),
        ],
        compiler_params=params(),
        name="filter",
    )(u_hi, u_lo, acc, sides, gpot.reshape(-1, LANES), xf, xb, bwd_m)


def solution(mesh):
    placed = (P("fn", None, None), P(), P("fn"), P(), P("fn"), P(), P())
    return jax.shard_map(
        body, mesh=mesh, in_specs=placed, out_specs=P("fn", None, None), check_vma=False
    )
```

```python
import functools

import jax
import jax.numpy as jnp
from jax import lax
from jax.experimental import pallas as pl
from jax.experimental.pallas import tpu as pltpu
from jax.sharding import PartitionSpec as P

NY = 64
NZ = 32
LANES = 128
SLAB = 256
YS = SLAB // NZ
GROUP = 4
VMEM = pl.BlockSpec(memory_space=pltpu.VMEM)
HBM = pl.BlockSpec(memory_space=pltpu.HBM)
F32 = jnp.float32
BF16 = jnp.bfloat16


def halves(values):
    high = values.astype(BF16)
    low = (values - high.astype(F32)).astype(BF16)
    return high, low


def dot(left, right):
    return jnp.dot(left, right, preferred_element_type=F32)


def params(**more):
    return pltpu.CompilerParams(vmem_limit_bytes=48 << 20, has_side_effects="collective_id" in more, **more)


def x_of(row, devices, spread):
    if spread == 1:
        return row
    return lax.rem(row, devices) * spread + row // devices


def matrices(devices, kin_ref, mag_ref, kx_out, kin_out, fwd_out, xf_ref, xb_ref, bwd_out):
    nx = xb_ref.shape[0]
    kin_half = kin_ref.shape[0]
    taps = mag_ref.shape[0]
    kin_count = 2 * kin_half - 1
    kin_center, mag_center = kin_count // 2, taps // 2
    kin = [-0.5 * kin_ref[abs(t - kin_center)] for t in range(kin_count)]
    mag = [mag_ref[t] for t in range(taps)]
    total = functools.reduce(lambda a, b: a + b, [jnp.abs(m) for m in mag])

    def picked(index, values, first=0):
        summed = jnp.zeros(index.shape, F32)
        for t, value in enumerate(values):
            summed = jnp.where(index == t + first, value, summed)
        return summed

    def iota(shape, dim):
        return lax.broadcasted_iota(jnp.int32, shape, dim)

    parts = kx_out.shape[0]
    plain = iota((nx, nx), 0)
    out_x, in_x = (x_of(iota((nx, nx), d), devices, parts) for d in (0, 1))
    ahead = lax.rem(in_x - out_x + mag_center + nx, nx)
    behind = lax.rem(plain - in_x + mag_center + nx, nx)
    across = lax.rem(in_x - plain + kin_center + nx, nx)
    fh, fl = halves(picked(ahead, mag) / total)
    kh, kl = halves(picked(across, kin))
    bh, bl = halves(picked(behind, mag) / total)
    xf_ref[...] = jnp.concatenate([fh, fl, fh], axis=1)
    xb_ref[...] = jnp.concatenate([bh, bl, bh], axis=1)
    each = nx // parts
    for part in range(parts):
        columns = slice(part * each, (part + 1) * each)
        kx_out[part] = jnp.concatenate([kh[:, columns], kl[:, columns], kh[:, columns]], axis=1)

    square = (SLAB, SLAB)
    row, col = iota(square, 0), iota(square, 1)
    in_y, in_z = row // NZ, lax.rem(row, NZ)
    out_y, out_z = col // NZ, lax.rem(col, NZ)
    dy, dz = in_y - out_y, in_z - out_z

    def along_y(delta, values, center, d):
        low = max(YS * d + center - (YS - 1), 0)
        high = min(YS * d + center + YS - 1, len(values) - 1)
        return picked(delta + (YS * d + center), values[low:high + 1], low)

    mag_z = picked(lax.rem(dz + mag_center + NZ, NZ), mag) / total
    mag_zt = picked(lax.rem(mag_center - dz + NZ, NZ), mag) / total
    kin_z = picked(lax.rem(dz + kin_center + NZ, NZ), kin)
    reach = fwd_out.shape[0] // 2 // SLAB // 2
    kin_reach = kin_out.shape[0] // 2 // SLAB // 2
    for n in range(2 * reach + 1):
        d = n - reach
        for out, y_part, z_part in (
            (fwd_out, along_y(dy, mag, mag_center, d), mag_z),
            (bwd_out, along_y(-dy, mag, mag_center, -d), mag_zt),
        ):
            high, low = halves(y_part / total * z_part)
            out[n * SLAB:(n + 1) * SLAB] = high
            base = (2 * reach + 1 + n) * SLAB
            out[base:base + SLAB] = low
    for n in range(2 * kin_reach + 1):
        d = n - kin_reach
        value = jnp.where(dz == 0, along_y(dy, kin, kin_center, d), 0.0)
        if d == 0:
            value = value + jnp.where(dy == 0, kin_z, 0.0)
        high, low = halves(value)
        kin_out[n * SLAB:(n + 1) * SLAB] = high
        base = (2 * kin_reach + 1 + n) * SLAB
        kin_out[base:base + SLAB] = low


def mixing_matrix(devices, counts_ref, kernel_ref, mix_out):
    functions = kernel_ref.shape[0]
    local = functions // devices
    full = (functions, functions)
    row, col = (lax.broadcasted_iota(jnp.int32, full, d) for d in (0, 1))
    lead = jnp.zeros((1, functions), jnp.int32)
    lane = lax.broadcasted_iota(jnp.int32, (1, functions), 1)
    pair = lane // (2 * local)
    for k in range(devices // 2):
        lead = jnp.where(pair == k, counts_ref[2 * k], lead)
    slot = lax.rem(lane, local)
    odd = lax.rem(lane // local, 2) == 1
    count = jnp.where(odd, 2 * local - lead, lead)
    first = jnp.where(odd, lead, 0)
    stand_in = jnp.where(odd, local, 2 * local - 1)
    second = jnp.where(count < local, stand_in, first + 1)
    place = pair * (2 * local) + jnp.where(slot == 0, first, second)
    wanted = lax.rem(row, devices) * local + row // devices
    row_pick = jnp.where(wanted == col, 1.0, 0.0).astype(BF16)
    col_pick = jnp.where(row == place, 1.0, 0.0).astype(BF16)
    parts = [dot(dot(row_pick, part).astype(BF16), col_pick).astype(BF16) for part in halves(kernel_ref[...])]
    mix_out[...] = jnp.concatenate([parts[0], parts[1], parts[0]], axis=1)


def partner(me, k):
    bit = 1
    there = me
    while bit <= k:
        if k & bit:
            there = there + bit - 2 * bit * ((me // bit) % 2)
        bit *= 2
    return there


def far_first(devices):
    half = devices // 2
    order = []
    for n in range(half):
        order += [half + n, n]
    return [k for k in order if k]


def remote(source, target, send, recv, device):
    return pltpu.make_async_remote_copy(
        src_ref=source, dst_ref=target, send_sem=send, recv_sem=recv,
        device_id=(device,), device_id_type=pl.DeviceIdType.MESH,
    )


def cube_root(x):
    guess = jnp.exp(jnp.log(x) * (1.0 / 3.0))
    return guess - (guess - x / (guess * guess)) * (1.0 / 3.0)


def banded(matrix_ref, high, low, slabs, wanted):
    width = matrix_ref.shape[0] // 2
    count = width // SLAB

    def wide(at):
        return jnp.concatenate([
            jnp.concatenate([at((h + n - count // 2) % slabs) for n in range(count)], axis=1) for h in wanted
        ], axis=0)

    high, low = wide(high), wide(low)
    return dot(high, matrix_ref[:width]) + (dot(low, matrix_ref[:width]) + dot(high, matrix_ref[width:]))


def exchange_kernel(devices, parts,
                    slots_hbm, shift_hbm, counts_hbm, kernel_hbm, external_hbm, kin_hbm, mag_hbm,
                    xf_ref, xb_ref, bwd_out, u_hi, u_lo, acc_ref, sides_ref, gpot_ref,
                    kx_ref, kin_out, fwd_out, v_hi, v_lo, back_ref, raw_ref, own_ref, out_ref, in_ref, got_ref, mixed_ref, pots_ref,
                    mix_ref, kernel_ref, external_ref, up_ref, down_ref,
                    shift_ref, counts_ref, kin_ref, mag_ref,
                    load_sem, swap_sem, lead_send, lead_recv, part_send, part_recv,
                    back_send, back_recv, pot_send, pot_recv):
    slot_each, nx, cells = raw_ref.shape
    functions = kernel_ref.shape[0]
    local = functions // devices
    q_count = cells // LANES
    rows_per = external_ref.shape[0]
    rows = rows_per // parts
    half = devices // 2
    count = functions // 2
    me = lax.axis_index("fn")
    side = me // half
    across = partner(me, half)
    mate = partner(me, 1)

    def load(source, target, k):
        copy = pltpu.make_async_copy(source, target, load_sem.at[k])
        copy.start()
        return copy

    slot_loads = {0: load(slots_hbm.at[0], raw_ref.at[0], 0)}
    shift_load = load(shift_hbm, shift_ref, slot_each)
    for s in reversed(range(1, slot_each)):
        slot_loads[s] = load(slots_hbm.at[s], raw_ref.at[s], s)
    barrier = pltpu.get_barrier_semaphore()
    for k in range(1, devices):
        pl.semaphore_signal(barrier, inc=1, device_id=(partner(me, k),), device_id_type=pl.DeviceIdType.MESH)
    order = far_first(devices)

    def block(part, device, field=0):
        return pl.multiple_of(((part * devices + device) * local + field) * rows, 8)

    spread = max(rows_per // q_count, 1)
    x_row = lax.broadcasted_iota(jnp.int32, (nx, nx), 0)
    x_col = lax.broadcasted_iota(jnp.int32, (nx, nx), 1)
    x_row = x_of(x_row, devices, spread)

    def rolled(s, target, fields, field):
        picked = lax.rem(x_row - shift_ref[s] + nx, nx) == x_col
        pick = jnp.where(picked, 1.0, 0.0).astype(BF16)
        pick = jnp.concatenate([pick, pick], axis=1)
        slot_loads[s].wait()
        for h in range(cells // SLAB):
            high, low = halves(raw_ref[s, :, h * SLAB:(h + 1) * SLAB])
            moved = dot(pick, jnp.concatenate([high, low], axis=0))
            for k in range(SLAB // LANES):
                q = h * (SLAB // LANES) + k
                column = moved[:, k * LANES:(k + 1) * LANES]
                if rows_per >= q_count:
                    for xo in range(spread):
                        at = xo * q_count + q
                        start = (at // rows * devices * fields + field) * rows + at % rows
                        target[pl.ds(start, devices, stride=fields * rows), :] = (
                            column[xo * devices:(xo + 1) * devices]
                        )
                else:
                    start = (q // rows * fields + field) * rows + q % rows
                    target[pl.ds(start, nx, stride=q_count // rows * fields * rows), :] = column

    shift_load.wait()
    rolled(0, own_ref, local, 0)
    pl.semaphore_wait(barrier, devices - 1)

    sends = []
    arrivals = [[] for _ in range(parts)]

    def give(part, first, fields, k, send, recv):
        there = partner(me, k)
        copy = remote(own_ref.at[pl.ds(block(part, there, first), fields * rows)],
                      got_ref.at[pl.ds(block(part, me, first), fields * rows)], send.at[k], recv.at[k], there)
        copy.start()
        sends.append(copy)
        arrivals[part].append(copy)

    for k in order:
        give(0, 0, 1, k, lead_send, lead_recv)
    last = slot_each - 1
    small = [load(a, b, slot_each + 1 + k) for k, (a, b) in enumerate((
        (counts_hbm, counts_ref), (kernel_hbm, kernel_ref), (external_hbm, external_ref),
        (kin_hbm, kin_ref), (mag_hbm, mag_ref),
    ))]
    rolled(last, out_ref, 1, 0)
    swap = remote(out_ref, in_ref, swap_sem.at[0], swap_sem.at[1], mate)
    swap.start()
    rolled(1, own_ref, local, 1)
    for copy in small:
        copy.wait()
    swap.wait_recv()
    lone = jnp.full((rows, LANES), counts_ref[me], jnp.int32) < local
    for part in range(parts):
        for dest in range(devices):
            where = ((part * devices + dest) * local + 1) * rows
            there = (part * devices + dest) * rows
            mine = own_ref[where:where + rows, :]
            own_ref[where:where + rows, :] = jnp.where(lone, in_ref[there:there + rows, :], mine)
    for k in order:
        give(0, 1, local - 1, k, part_send.at[0], part_recv.at[0])
    for part in range(1, parts):
        for k in order:
            give(part, 0, local, k, part_send.at[part], part_recv.at[part])
    for part in range(parts):
        got_ref[pl.ds(block(part, me), local * rows), :] = own_ref[pl.ds(block(part, me), local * rows), :]

    mixing_matrix(devices, counts_ref, kernel_ref, mix_ref)
    matrices(devices, kin_ref, mag_ref, kx_ref, kin_out, fwd_out, xf_ref, xb_ref, bwd_out)
    acc_ref[...] = jnp.zeros_like(acc_ref)
    sides = jnp.abs(kin_ref[0])
    for t in range(1, kin_ref.shape[0]):
        sides = sides + 2.0 * jnp.abs(kin_ref[t])
    sides_ref[...] = jnp.full(sides_ref.shape, 1.0 + 1.5 * sides, F32)
    slabs = cells // SLAB
    per_slab = SLAB // LANES
    each = nx // parts
    split = max(q_count // rows, 1)

    def forward(part, first, n):
        group = GROUP
        length = n * split * local * rows
        begin = pl.multiple_of((part * devices + first * split) * local * rows, 8)
        view = back_ref.at[pl.ds(begin, length)]

        def where(f):
            return pl.ds(pl.multiple_of((part * local + f) * each + first, 16), n)

        for h in range(slabs):
            for f in range(local):
                value = jnp.concatenate([
                    view[pl.ds((q // rows * local + f) * rows + q % rows, n, stride=split * local * rows), :]
                    for q in range(h * per_slab, (h + 1) * per_slab)
                ], axis=1)
                v_hi[h, where(f)], v_lo[h, where(f)] = halves(value)

        def at(ref):
            return lambda h: jnp.concatenate([ref[h, where(f)] for f in range(local)], axis=0)

        for step in range(0, slabs, group):
            wanted = range(step, step + group)
            kinetic = banded(kin_out, at(v_hi), at(v_lo), slabs, wanted)
            smooth = banded(fwd_out, at(v_hi), at(v_lo), slabs, wanted)
            for g, h in enumerate(wanted):
                for f in range(local):
                    base = (g * local + f) * n
                    u_hi[h, where(f)], u_lo[h, where(f)] = halves(smooth[base:base + n])
                    rows_at = pl.ds(pl.multiple_of(f * nx + first * parts, 8), n * parts)
                    for k in range(per_slab):
                        target = acc_ref.at[h * per_slab + k, rows_at]
                        some = pl.ds(part, n, stride=parts) if parts > 1 else slice(None)
                        target[some, :] += kinetic[base:base + n, k * LANES:(k + 1) * LANES]

    def along_x(part):
        for h in range(slabs):
            for f in range(local):
                here = slice((part * local + f) * each, (part * local + f + 1) * each)
                high, low = v_hi[h, here], v_lo[h, here]
                moved = dot(kx_ref[part], jnp.concatenate([high, high, low], axis=0))
                for k in range(per_slab):
                    acc_ref[h * per_slab + k, f * nx:(f + 1) * nx, :] += moved[:, k * LANES:(k + 1) * LANES]

    def mix(part):
        base = part * functions * rows
        for c in range(0, rows, 2):
            values = jnp.concatenate(
                [got_ref[pl.ds(base + c + k, functions, stride=rows), :] for k in range(2)], axis=1
            )
            high, low = halves(values)
            mixed = dot(mix_ref[...], jnp.concatenate([high, high, low], axis=0))
            up = down = 0.0
            for j in range(local):
                piece = mixed[j * devices:(j + 1) * devices]
                for k in range(2):
                    mixed_ref[pl.ds(base + j * rows + c + k, devices, stride=local * rows), :] = (
                        piece[:, k * LANES:(k + 1) * LANES]
                    )
                squared = piece * piece
                up = up + jnp.sum(squared[:half], axis=0, keepdims=True)
                down = down + jnp.sum(squared[half:], axis=0, keepdims=True)
            for k in range(2):
                up_ref[c + k:c + k + 1, :] = up[:, k * LANES:(k + 1) * LANES]
                down_ref[c + k:c + k + 1, :] = down[:, k * LANES:(k + 1) * LANES]
        rho_up, rho_down = up_ref[...] / count, down_ref[...] / count
        shared = external_ref[part * rows:(part + 1) * rows, :] + 0.5 * (rho_up + rho_down)
        spins = [shared - cube_root((6.0 / jnp.pi) * rho + 1e-6) for rho in (rho_up, rho_down)]
        for spin in range(2):
            pots_ref[spin, part * rows:(part + 1) * rows] = spins[spin]
        sizes = jnp.maximum(jnp.abs(spins[0]), jnp.abs(spins[1]))
        peak = sizes[:8]
        for w in range(1, rows // 8):
            peak = jnp.maximum(peak, sizes[w * 8:(w + 1) * 8])
        return peak

    peak = None
    returns, waits = [[] for _ in range(parts)], []
    for part in range(parts):
        for copy in arrivals[part]:
            copy.wait_recv()
        here = mix(part)
        peak = here if peak is None else jnp.maximum(peak, here)
        begin, extent = part * rows, rows
        if part == parts - 1:
            extent = rows + 1
            for spin in range(2):
                pots_ref[spin, rows_per:rows_per + 1] = jnp.max(peak, axis=0, keepdims=True)
        span = pl.ds(begin, extent)

        def show(source, owner, slot, there):
            copy = remote(source, gpot_ref.at[owner, span], pot_send.at[part, slot], pot_recv.at[part, slot], there)
            copy.start()
            return copy

        handed = show(pots_ref.at[1 - side, span], me, 0, across)
        sends.append(handed)
        for k in range(1, half):
            waits.append(show(pots_ref.at[side, span], me, k, partner(me, k)))
        for k in order:
            there = partner(me, k)
            copy = remote(mixed_ref.at[pl.ds(block(part, there), local * rows)],
                          back_ref.at[pl.ds(block(part, me), local * rows)],
                          back_send.at[part, k], back_recv.at[part, k], there)
            copy.start()
            returns[part].append((k, copy))
        back_ref[pl.ds(block(part, me), local * rows), :] = mixed_ref[pl.ds(block(part, me), local * rows), :]
        gpot_ref[me, begin:begin + extent] = pots_ref[side, begin:begin + extent]
        handed.wait_recv()
        for k in range(1, half):
            waits.append(show(gpot_ref.at[across, span], across, half + k, partner(me, k)))

    for copy in [swap, *sends]:
        copy.wait_send()
    for part in range(parts - 1):
        for _, copy in returns[part]:
            copy.wait_recv()
        forward(part, 0, each)
        for _, copy in returns[part]:
            copy.wait_send()
        along_x(part)
    final = parts - 1
    late = waits[1 - half:]
    for copy in waits[:1 - half]:
        copy.wait()
    for near in (True, False):
        for k, copy in returns[final]:
            if (k < half) == near:
                copy.wait_recv()
        forward(final, (side if near else 1 - side) * (each // 2), each // 2)
    along_x(final)
    for copy in late:
        copy.wait_recv()
    for copy in [*late, *(copy for _, copy in returns[final])]:
        copy.wait_send()


def filter_kernel(devices, rows_per, u_hi, u_lo, acc_ref, sides_ref, gpot_ref, xf_ref, xb_ref, bwd_ref, out_hbm,
                  w_hi, w_lo, out_ref, out_sem):
    local, nx, cells = out_ref.shape
    slabs = cells // SLAB
    q_count = cells // LANES
    per_slab = SLAB // LANES
    parts = max(rows_per // q_count, 1)
    each = nx // parts
    pot_rows = gpot_ref.shape[0] // devices

    def plane(q):
        if rows_per >= q_count:
            return jnp.concatenate([
                gpot_ref[pl.ds(xo * q_count + q, devices, stride=pot_rows), :] for xo in range(parts)
            ], axis=0)
        split = q_count // rows_per
        return gpot_ref[pl.ds((q // rows_per) * pot_rows + q % rows_per, nx, stride=split * pot_rows), :]

    peaks = gpot_ref[pl.ds(rows_per, devices, stride=pot_rows), :]
    bound = sides_ref[:1, :] + jnp.max(peaks)
    scale = jnp.concatenate([1.0 / bound] * per_slab, axis=1)

    for h in range(slabs):
        potential = jnp.concatenate([plane(h * per_slab + k) for k in range(per_slab)], axis=1)
        for f in range(local):
            def taken(ref):
                starts = [(part * local + f) * each for part in range(parts)]
                return jnp.concatenate([ref[h, start:start + each] for start in starts], axis=0)

            high, low = taken(u_hi), taken(u_lo)
            smooth = dot(xf_ref[...], jnp.concatenate([high, high, low], axis=0))
            high, low = halves(smooth * potential)
            moved = dot(xb_ref[...], jnp.concatenate([high, high, low], axis=0))
            w_hi[h, f * nx:(f + 1) * nx], w_lo[h, f * nx:(f + 1) * nx] = halves(moved)

    copies = []
    group = slabs // out_sem.shape[0]
    for step in range(0, slabs, group):
        wanted = range(step, step + group)
        back = banded(bwd_ref, lambda h: w_hi[h], lambda h: w_lo[h], slabs, wanted)
        for g, h in enumerate(wanted):
            kinetic = jnp.concatenate([acc_ref[h * per_slab + k] for k in range(per_slab)], axis=1)
            result = (kinetic + back[g * local * nx:(g + 1) * local * nx]) * scale
            for f in range(local):
                out_ref[f, :, h * SLAB:(h + 1) * SLAB] = result[f * nx:(f + 1) * nx]
        columns = pl.ds(step * SLAB, group * SLAB)
        copy = pltpu.make_async_copy(out_ref.at[:, :, columns], out_hbm.at[:, :, columns], out_sem.at[len(copies)])
        copy.start()
        copies.append(copy)
    for copy in copies:
        copy.wait()


def shaped(shape, dtype=F32):
    return jax.ShapeDtypeStruct(shape, dtype)


def body(support_functions, owner_counts, region_shift, kernel, external, kinetic_taps, magic_taps):
    devices = lax.axis_size("fn")
    slot_each, nx, cells = support_functions.shape
    functions = kernel.shape[0]
    local = functions // devices
    rows_per = nx * cells // devices // LANES
    q_count = cells // LANES
    parts = max(rows_per // q_count, 1)
    rows = rows_per // parts
    reach = -(-(magic_taps.shape[0] // 2) // YS)
    kin_reach = -(-(kinetic_taps.shape[0] - 1) // YS)

    each = pltpu.SemaphoreType.DMA((devices,))
    each_part = pltpu.SemaphoreType.DMA((parts, devices))
    flat = (nx * q_count, LANES)
    whole = (functions * rows_per, LANES)
    slabs = cells // SLAB
    tile = (slabs, local * nx, SLAB)
    kin_band = pltpu.VMEM((2 * (2 * kin_reach + 1) * SLAB, SLAB), BF16)
    mag_band = (2 * (2 * reach + 1) * SLAB, SLAB)
    xf, xb, bwd_m, u_hi, u_lo, acc, sides, gpot = pl.pallas_call(
        functools.partial(exchange_kernel, devices, parts),
        out_shape=(
            shaped((nx, 3 * nx), BF16),
            shaped((nx, 3 * nx), BF16),
            shaped(mag_band, BF16),
            shaped(tile, BF16),
            shaped(tile, BF16),
            shaped((q_count, local * nx, LANES)),
            shaped((8, LANES)),
            shaped((devices, rows_per + 8, LANES)),
        ),
        in_specs=[HBM] * 7,
        out_specs=(VMEM,) * 8,
        scratch_shapes=[
            pltpu.VMEM((parts, nx, 3 * nx // parts), BF16), kin_band, pltpu.VMEM(mag_band, BF16),
            pltpu.VMEM(tile, BF16), pltpu.VMEM(tile, BF16), pltpu.VMEM(whole, F32),
            pltpu.VMEM((slot_each, nx, cells), F32), pltpu.VMEM(whole, F32),
            pltpu.VMEM(flat, F32), pltpu.VMEM(flat, F32), pltpu.VMEM(whole, F32), pltpu.VMEM(whole, F32),
            pltpu.VMEM((2, rows_per + 8, LANES), F32), pltpu.VMEM((functions, 3 * functions), BF16),
            pltpu.VMEM((functions, functions), F32), pltpu.VMEM((rows_per, LANES), F32),
            pltpu.VMEM((rows, LANES), F32), pltpu.VMEM((rows, LANES), F32),
            pltpu.SMEM(region_shift.shape, jnp.int32), pltpu.SMEM(owner_counts.shape, jnp.int32),
            pltpu.SMEM(kinetic_taps.shape, F32), pltpu.SMEM(magic_taps.shape, F32),
            pltpu.SemaphoreType.DMA((slot_each + 6,)), pltpu.SemaphoreType.DMA((2,)), each, each,
        ] + [each_part] * 6,
        compiler_params=params(collective_id=0),
        name="exchange",
    )(*(pltpu.with_memory_space_constraint(x, pltpu.HBM) for x in (
        support_functions, region_shift, owner_counts, kernel, external.reshape(rows_per, LANES),
        kinetic_taps, magic_taps,
    )))

    return pl.pallas_call(
        functools.partial(filter_kernel, devices, rows_per),
        out_shape=shaped((local, nx, cells)),
        in_specs=[VMEM] * 8,
        out_specs=HBM,
        scratch_shapes=[
            pltpu.VMEM(tile, BF16), pltpu.VMEM(tile, BF16), pltpu.VMEM((local, nx, cells), F32),
            pltpu.SemaphoreType.DMA((4,)),
        ],
        compiler_params=params(),
        name="filter",
    )(u_hi, u_lo, acc, sides, gpot.reshape(-1, LANES), xf, xb, bwd_m)


def solution(mesh):
    placed = (P("fn", None, None), P(), P("fn"), P(), P("fn"), P(), P())
    return jax.shard_map(
        body, mesh=mesh, in_specs=placed, out_specs=P("fn", None, None), check_vma=False
    )
```

```python
import functools

import jax
import jax.numpy as jnp
from jax import lax
from jax.experimental import pallas as pl
from jax.experimental.pallas import tpu as pltpu
from jax.sharding import PartitionSpec as P

NY = 64
NZ = 32
LANES = 128
SLAB = 256
YS = SLAB // NZ
GROUP = 4
VMEM = pl.BlockSpec(memory_space=pltpu.VMEM)
HBM = pl.BlockSpec(memory_space=pltpu.HBM)
F32 = jnp.float32
BF16 = jnp.bfloat16


def halves(values):
    high = values.astype(BF16)
    low = (values - high.astype(F32)).astype(BF16)
    return high, low


def dot(left, right):
    return jnp.dot(left, right, preferred_element_type=F32)


def params(**more):
    return pltpu.CompilerParams(vmem_limit_bytes=48 << 20, has_side_effects="collective_id" in more, **more)


def x_of(row, devices, spread):
    if spread == 1:
        return row
    return lax.rem(row, devices) * spread + row // devices


def matrices(devices, kin_ref, mag_ref, kx_out, kin_out, fwd_out, xf_ref, xb_ref, bwd_out):
    nx = xb_ref.shape[0]
    kin_half = kin_ref.shape[0]
    taps = mag_ref.shape[0]
    kin_count = 2 * kin_half - 1
    kin_center, mag_center = kin_count // 2, taps // 2
    kin = [-0.5 * kin_ref[abs(t - kin_center)] for t in range(kin_count)]
    mag = [mag_ref[t] for t in range(taps)]
    total = functools.reduce(lambda a, b: a + b, [jnp.abs(m) for m in mag])

    def picked(index, values, first=0):
        summed = jnp.zeros(index.shape, F32)
        for t, value in enumerate(values):
            summed = jnp.where(index == t + first, value, summed)
        return summed

    def iota(shape, dim):
        return lax.broadcasted_iota(jnp.int32, shape, dim)

    parts = kx_out.shape[0]
    plain = iota((nx, nx), 0)
    out_x, in_x = (x_of(iota((nx, nx), d), devices, parts) for d in (0, 1))
    ahead = lax.rem(in_x - out_x + mag_center + nx, nx)
    behind = lax.rem(plain - in_x + mag_center + nx, nx)
    across = lax.rem(in_x - plain + kin_center + nx, nx)
    fh, fl = halves(picked(ahead, mag) / total)
    kh, kl = halves(picked(across, kin))
    bh, bl = halves(picked(behind, mag) / total)
    xf_ref[...] = jnp.concatenate([fh, fl, fh], axis=1)
    xb_ref[...] = jnp.concatenate([bh, bl, bh], axis=1)
    each = nx // parts
    for part in range(parts):
        columns = slice(part * each, (part + 1) * each)
        kx_out[part] = jnp.concatenate([kh[:, columns], kl[:, columns], kh[:, columns]], axis=1)

    square = (SLAB, SLAB)
    row, col = iota(square, 0), iota(square, 1)
    in_y, in_z = row // NZ, lax.rem(row, NZ)
    out_y, out_z = col // NZ, lax.rem(col, NZ)
    dy, dz = in_y - out_y, in_z - out_z

    def along_y(delta, values, center, d):
        low = max(YS * d + center - (YS - 1), 0)
        high = min(YS * d + center + YS - 1, len(values) - 1)
        return picked(delta + (YS * d + center), values[low:high + 1], low)

    mag_z = picked(lax.rem(dz + mag_center + NZ, NZ), mag) / total
    mag_zt = picked(lax.rem(mag_center - dz + NZ, NZ), mag) / total
    kin_z = picked(lax.rem(dz + kin_center + NZ, NZ), kin)
    reach = fwd_out.shape[0] // 2 // SLAB // 2
    kin_reach = kin_out.shape[0] // 2 // SLAB // 2
    for n in range(2 * reach + 1):
        d = n - reach
        for out, y_part, z_part in (
            (fwd_out, along_y(dy, mag, mag_center, d), mag_z),
            (bwd_out, along_y(-dy, mag, mag_center, -d), mag_zt),
        ):
            high, low = halves(y_part / total * z_part)
            out[n * SLAB:(n + 1) * SLAB] = high
            base = (2 * reach + 1 + n) * SLAB
            out[base:base + SLAB] = low
    for n in range(2 * kin_reach + 1):
        d = n - kin_reach
        value = jnp.where(dz == 0, along_y(dy, kin, kin_center, d), 0.0)
        if d == 0:
            value = value + jnp.where(dy == 0, kin_z, 0.0)
        high, low = halves(value)
        kin_out[n * SLAB:(n + 1) * SLAB] = high
        base = (2 * kin_reach + 1 + n) * SLAB
        kin_out[base:base + SLAB] = low


def mixing_matrix(devices, counts_ref, kernel_ref, mix_out):
    functions = kernel_ref.shape[0]
    local = functions // devices
    full = (functions, functions)
    row, col = (lax.broadcasted_iota(jnp.int32, full, d) for d in (0, 1))
    lead = jnp.zeros((1, functions), jnp.int32)
    lane = lax.broadcasted_iota(jnp.int32, (1, functions), 1)
    pair = lane // (2 * local)
    for k in range(devices // 2):
        lead = jnp.where(pair == k, counts_ref[2 * k], lead)
    slot = lax.rem(lane, local)
    odd = lax.rem(lane // local, 2) == 1
    count = jnp.where(odd, 2 * local - lead, lead)
    first = jnp.where(odd, lead, 0)
    stand_in = jnp.where(odd, local, 2 * local - 1)
    second = jnp.where(count < local, stand_in, first + 1)
    place = pair * (2 * local) + jnp.where(slot == 0, first, second)
    wanted = lax.rem(row, devices) * local + row // devices
    row_pick = jnp.where(wanted == col, 1.0, 0.0).astype(BF16)
    col_pick = jnp.where(row == place, 1.0, 0.0).astype(BF16)
    parts = [dot(dot(row_pick, part).astype(BF16), col_pick).astype(BF16) for part in halves(kernel_ref[...])]
    mix_out[...] = jnp.concatenate([parts[0], parts[1], parts[0]], axis=1)


def partner(me, k):
    bit = 1
    there = me
    while bit <= k:
        if k & bit:
            there = there + bit - 2 * bit * ((me // bit) % 2)
        bit *= 2
    return there


def far_first(devices):
    half = devices // 2
    order = []
    for n in range(half):
        order += [half + n, n]
    return [k for k in order if k]


def remote(source, target, send, recv, device):
    return pltpu.make_async_remote_copy(
        src_ref=source, dst_ref=target, send_sem=send, recv_sem=recv,
        device_id=(device,), device_id_type=pl.DeviceIdType.MESH,
    )


def cube_root(x):
    guess = jnp.exp(jnp.log(x) * (1.0 / 3.0))
    return guess - (guess - x / (guess * guess)) * (1.0 / 3.0)


def banded(matrix_ref, high, low, slabs, wanted):
    width = matrix_ref.shape[0] // 2
    count = width // SLAB

    def wide(at):
        return jnp.concatenate([
            jnp.concatenate([at((h + n - count // 2) % slabs) for n in range(count)], axis=1) for h in wanted
        ], axis=0)

    high, low = wide(high), wide(low)
    return dot(high, matrix_ref[:width]) + (dot(low, matrix_ref[:width]) + dot(high, matrix_ref[width:]))


def exchange_kernel(devices, parts,
                    slots_hbm, shift_hbm, counts_hbm, kernel_hbm, external_hbm, kin_hbm, mag_hbm,
                    xf_ref, xb_ref, bwd_out, u_hi, u_lo, acc_ref, sides_ref, gpot_ref,
                    kx_ref, kin_out, fwd_out, v_hi, v_lo, back_ref, raw_ref, own_ref, out_ref, in_ref, got_ref, mixed_ref, pots_ref,
                    mix_ref, kernel_ref, external_ref, up_ref, down_ref,
                    shift_ref, counts_ref, kin_ref, mag_ref,
                    load_sem, swap_sem, lead_send, lead_recv, part_send, part_recv,
                    back_send, back_recv, pot_send, pot_recv):
    slot_each, nx, cells = raw_ref.shape
    functions = kernel_ref.shape[0]
    local = functions // devices
    q_count = cells // LANES
    rows_per = external_ref.shape[0]
    rows = rows_per // parts
    half = devices // 2
    count = functions // 2
    me = lax.axis_index("fn")
    side = me // half
    across = partner(me, half)
    mate = partner(me, 1)

    def load(source, target, k):
        copy = pltpu.make_async_copy(source, target, load_sem.at[k])
        copy.start()
        return copy

    slot_loads = {0: load(slots_hbm.at[0], raw_ref.at[0], 0)}
    shift_load = load(shift_hbm, shift_ref, slot_each)
    for s in reversed(range(1, slot_each)):
        slot_loads[s] = load(slots_hbm.at[s], raw_ref.at[s], s)
    barrier = pltpu.get_barrier_semaphore()
    for k in range(1, devices):
        pl.semaphore_signal(barrier, inc=1, device_id=(partner(me, k),), device_id_type=pl.DeviceIdType.MESH)
    order = far_first(devices)

    def block(part, device, field=0):
        return pl.multiple_of(((part * devices + device) * local + field) * rows, 8)

    spread = max(rows_per // q_count, 1)
    x_row = lax.broadcasted_iota(jnp.int32, (nx, nx), 0)
    x_col = lax.broadcasted_iota(jnp.int32, (nx, nx), 1)
    x_row = x_of(x_row, devices, spread)

    def rolled(s, target, fields, field):
        picked = lax.rem(x_row - shift_ref[s] + nx, nx) == x_col
        pick = jnp.where(picked, 1.0, 0.0).astype(BF16)
        pick = jnp.concatenate([pick, pick], axis=1)
        slot_loads[s].wait()
        for h in range(cells // SLAB):
            high, low = halves(raw_ref[s, :, h * SLAB:(h + 1) * SLAB])
            moved = dot(pick, jnp.concatenate([high, low], axis=0))
            for k in range(SLAB // LANES):
                q = h * (SLAB // LANES) + k
                column = moved[:, k * LANES:(k + 1) * LANES]
                if rows_per >= q_count:
                    for xo in range(spread):
                        at = xo * q_count + q
                        start = (at // rows * devices * fields + field) * rows + at % rows
                        target[pl.ds(start, devices, stride=fields * rows), :] = (
                            column[xo * devices:(xo + 1) * devices]
                        )
                else:
                    start = (q // rows * fields + field) * rows + q % rows
                    target[pl.ds(start, nx, stride=q_count // rows * fields * rows), :] = column

    shift_load.wait()
    rolled(0, own_ref, local, 0)
    pl.semaphore_wait(barrier, devices - 1)

    sends = []
    arrivals = [[] for _ in range(parts)]

    def give(part, first, fields, k, send, recv):
        there = partner(me, k)
        copy = remote(own_ref.at[pl.ds(block(part, there, first), fields * rows)],
                      got_ref.at[pl.ds(block(part, me, first), fields * rows)], send.at[k], recv.at[k], there)
        copy.start()
        sends.append(copy)
        arrivals[part].append(copy)

    for k in order:
        give(0, 0, 1, k, lead_send, lead_recv)
    last = slot_each - 1
    small = [load(a, b, slot_each + 1 + k) for k, (a, b) in enumerate((
        (counts_hbm, counts_ref), (kernel_hbm, kernel_ref), (external_hbm, external_ref),
        (kin_hbm, kin_ref), (mag_hbm, mag_ref),
    ))]
    rolled(last, out_ref, 1, 0)
    swap = remote(out_ref, in_ref, swap_sem.at[0], swap_sem.at[1], mate)
    swap.start()
    rolled(1, own_ref, local, 1)
    for copy in small:
        copy.wait()
    swap.wait_recv()
    lone = jnp.full((rows, LANES), counts_ref[me], jnp.int32) < local
    for part in range(parts):
        for dest in range(devices):
            where = ((part * devices + dest) * local + 1) * rows
            there = (part * devices + dest) * rows
            mine = own_ref[where:where + rows, :]
            own_ref[where:where + rows, :] = jnp.where(lone, in_ref[there:there + rows, :], mine)
    for k in order:
        give(0, 1, local - 1, k, part_send.at[0], part_recv.at[0])
    for part in range(1, parts):
        for k in order:
            give(part, 0, local, k, part_send.at[part], part_recv.at[part])
    for part in range(parts):
        got_ref[pl.ds(block(part, me), local * rows), :] = own_ref[pl.ds(block(part, me), local * rows), :]

    mixing_matrix(devices, counts_ref, kernel_ref, mix_ref)
    matrices(devices, kin_ref, mag_ref, kx_ref, kin_out, fwd_out, xf_ref, xb_ref, bwd_out)
    acc_ref[...] = jnp.zeros_like(acc_ref)
    sides = jnp.abs(kin_ref[0])
    for t in range(1, kin_ref.shape[0]):
        sides = sides + 2.0 * jnp.abs(kin_ref[t])
    sides_ref[...] = jnp.full(sides_ref.shape, 1.0 + 1.5 * sides, F32)
    slabs = cells // SLAB
    per_slab = SLAB // LANES
    each = nx // parts
    split = max(q_count // rows, 1)

    def forward(part, first, n):
        group = GROUP
        length = n * split * local * rows
        begin = pl.multiple_of((part * devices + first * split) * local * rows, 8)
        view = back_ref.at[pl.ds(begin, length)]

        def where(f):
            return pl.ds(pl.multiple_of((part * local + f) * each + first, 16), n)

        for h in range(slabs):
            for f in range(local):
                value = jnp.concatenate([
                    view[pl.ds((q // rows * local + f) * rows + q % rows, n, stride=split * local * rows), :]
                    for q in range(h * per_slab, (h + 1) * per_slab)
                ], axis=1)
                v_hi[h, where(f)], v_lo[h, where(f)] = halves(value)

        def at(ref):
            return lambda h: jnp.concatenate([ref[h, where(f)] for f in range(local)], axis=0)

        for step in range(0, slabs, group):
            wanted = range(step, step + group)
            kinetic = banded(kin_out, at(v_hi), at(v_lo), slabs, wanted)
            smooth = banded(fwd_out, at(v_hi), at(v_lo), slabs, wanted)
            for g, h in enumerate(wanted):
                for f in range(local):
                    base = (g * local + f) * n
                    u_hi[h, where(f)], u_lo[h, where(f)] = halves(smooth[base:base + n])
                    rows_at = pl.ds(pl.multiple_of(f * nx + first * parts, 8), n * parts)
                    for k in range(per_slab):
                        target = acc_ref.at[h * per_slab + k, rows_at]
                        some = pl.ds(part, n, stride=parts) if parts > 1 else slice(None)
                        target[some, :] += kinetic[base:base + n, k * LANES:(k + 1) * LANES]

    def along_x(part):
        for h in range(slabs):
            for f in range(local):
                here = slice((part * local + f) * each, (part * local + f + 1) * each)
                high, low = v_hi[h, here], v_lo[h, here]
                moved = dot(kx_ref[part], jnp.concatenate([high, high, low], axis=0))
                for k in range(per_slab):
                    acc_ref[h * per_slab + k, f * nx:(f + 1) * nx, :] += moved[:, k * LANES:(k + 1) * LANES]

    def mix(part):
        base = part * functions * rows
        for c in range(0, rows, 2):
            values = jnp.concatenate(
                [got_ref[pl.ds(base + c + k, functions, stride=rows), :] for k in range(2)], axis=1
            )
            high, low = halves(values)
            mixed = dot(mix_ref[...], jnp.concatenate([high, high, low], axis=0))
            up = down = 0.0
            for j in range(local):
                piece = mixed[j * devices:(j + 1) * devices]
                for k in range(2):
                    mixed_ref[pl.ds(base + j * rows + c + k, devices, stride=local * rows), :] = (
                        piece[:, k * LANES:(k + 1) * LANES]
                    )
                squared = piece * piece
                up = up + jnp.sum(squared[:half], axis=0, keepdims=True)
                down = down + jnp.sum(squared[half:], axis=0, keepdims=True)
            for k in range(2):
                up_ref[c + k:c + k + 1, :] = up[:, k * LANES:(k + 1) * LANES]
                down_ref[c + k:c + k + 1, :] = down[:, k * LANES:(k + 1) * LANES]
        rho_up, rho_down = up_ref[...] / count, down_ref[...] / count
        shared = external_ref[part * rows:(part + 1) * rows, :] + 0.5 * (rho_up + rho_down)
        spins = [shared - cube_root((6.0 / jnp.pi) * rho + 1e-6) for rho in (rho_up, rho_down)]
        for spin in range(2):
            pots_ref[spin, part * rows:(part + 1) * rows] = spins[spin]
        sizes = jnp.maximum(jnp.abs(spins[0]), jnp.abs(spins[1]))
        peak = sizes[:8]
        for w in range(1, rows // 8):
            peak = jnp.maximum(peak, sizes[w * 8:(w + 1) * 8])
        return peak

    peak = None
    returns, waits = [[] for _ in range(parts)], []
    for part in range(parts):
        for copy in arrivals[part]:
            copy.wait_recv()
        here = mix(part)
        peak = here if peak is None else jnp.maximum(peak, here)
        begin, extent = part * rows, rows
        if part == parts - 1:
            extent = rows + 1
            for spin in range(2):
                pots_ref[spin, rows_per:rows_per + 1] = jnp.max(peak, axis=0, keepdims=True)
        span = pl.ds(begin, extent)

        def show(source, owner, slot, there):
            copy = remote(source, gpot_ref.at[owner, span], pot_send.at[part, slot], pot_recv.at[part, slot], there)
            copy.start()
            return copy

        handed = show(pots_ref.at[1 - side, span], me, 0, across)
        sends.append(handed)
        for k in range(1, half):
            waits.append(show(pots_ref.at[side, span], me, k, partner(me, k)))
        for k in order:
            there = partner(me, k)
            copy = remote(mixed_ref.at[pl.ds(block(part, there), local * rows)],
                          back_ref.at[pl.ds(block(part, me), local * rows)],
                          back_send.at[part, k], back_recv.at[part, k], there)
            copy.start()
            returns[part].append((k, copy))
        back_ref[pl.ds(block(part, me), local * rows), :] = mixed_ref[pl.ds(block(part, me), local * rows), :]
        gpot_ref[me, begin:begin + extent] = pots_ref[side, begin:begin + extent]
        handed.wait_recv()
        for k in range(1, half):
            waits.append(show(gpot_ref.at[across, span], across, half + k, partner(me, k)))

    for copy in [swap, *sends]:
        copy.wait_send()
    for part in range(parts - 1):
        for _, copy in returns[part]:
            copy.wait_recv()
        forward(part, 0, each)
        for _, copy in returns[part]:
            copy.wait_send()
        along_x(part)
    final = parts - 1
    late = waits[1 - half:]
    for copy in waits[:1 - half]:
        copy.wait()
    for near in (True, False):
        for k, copy in returns[final]:
            if (k < half) == near:
                copy.wait_recv()
        forward(final, (side if near else 1 - side) * (each // 2), each // 2)
    along_x(final)
    for copy in late:
        copy.wait_recv()
    for copy in [*late, *(copy for _, copy in returns[final])]:
        copy.wait_send()


def filter_kernel(devices, rows_per, u_hi, u_lo, acc_ref, sides_ref, gpot_ref, xf_ref, xb_ref, bwd_ref, out_hbm,
                  w_hi, w_lo, out_ref, out_sem):
    local, nx, cells = out_ref.shape
    slabs = cells // SLAB
    q_count = cells // LANES
    per_slab = SLAB // LANES
    parts = max(rows_per // q_count, 1)
    each = nx // parts
    pot_rows = gpot_ref.shape[0] // devices

    def plane(q):
        if rows_per >= q_count:
            return jnp.concatenate([
                gpot_ref[pl.ds(xo * q_count + q, devices, stride=pot_rows), :] for xo in range(parts)
            ], axis=0)
        split = q_count // rows_per
        return gpot_ref[pl.ds((q // rows_per) * pot_rows + q % rows_per, nx, stride=split * pot_rows), :]

    peaks = gpot_ref[pl.ds(rows_per, devices, stride=pot_rows), :]
    bound = sides_ref[:1, :] + jnp.max(peaks)
    scale = jnp.concatenate([1.0 / bound] * per_slab, axis=1)

    for h in range(slabs):
        potential = jnp.concatenate([plane(h * per_slab + k) for k in range(per_slab)], axis=1)
        for f in range(local):
            def taken(ref):
                starts = [(part * local + f) * each for part in range(parts)]
                return jnp.concatenate([ref[h, start:start + each] for start in starts], axis=0)

            high, low = taken(u_hi), taken(u_lo)
            smooth = dot(xf_ref[...], jnp.concatenate([high, high, low], axis=0))
            high, low = halves(smooth * potential)
            moved = dot(xb_ref[...], jnp.concatenate([high, high, low], axis=0))
            w_hi[h, f * nx:(f + 1) * nx], w_lo[h, f * nx:(f + 1) * nx] = halves(moved)

    copies = []
    step = 0
    for group in [2] * (slabs // 2 - 1) + [1, 1]:
        wanted = range(step, step + group)
        back = banded(bwd_ref, lambda h: w_hi[h], lambda h: w_lo[h], slabs, wanted)
        for g, h in enumerate(wanted):
            kinetic = jnp.concatenate([acc_ref[h * per_slab + k] for k in range(per_slab)], axis=1)
            result = (kinetic + back[g * local * nx:(g + 1) * local * nx]) * scale
            for f in range(local):
                out_ref[f, :, h * SLAB:(h + 1) * SLAB] = result[f * nx:(f + 1) * nx]
        columns = pl.ds(step * SLAB, group * SLAB)
        copy = pltpu.make_async_copy(out_ref.at[:, :, columns], out_hbm.at[:, :, columns], out_sem.at[len(copies)])
        copy.start()
        copies.append(copy)
        step += group
    for copy in copies:
        copy.wait()


def shaped(shape, dtype=F32):
    return jax.ShapeDtypeStruct(shape, dtype)


def body(support_functions, owner_counts, region_shift, kernel, external, kinetic_taps, magic_taps):
    devices = lax.axis_size("fn")
    slot_each, nx, cells = support_functions.shape
    functions = kernel.shape[0]
    local = functions // devices
    rows_per = nx * cells // devices // LANES
    q_count = cells // LANES
    parts = max(rows_per // q_count, 1)
    rows = rows_per // parts
    reach = -(-(magic_taps.shape[0] // 2) // YS)
    kin_reach = -(-(kinetic_taps.shape[0] - 1) // YS)

    each = pltpu.SemaphoreType.DMA((devices,))
    each_part = pltpu.SemaphoreType.DMA((parts, devices))
    flat = (nx * q_count, LANES)
    whole = (functions * rows_per, LANES)
    slabs = cells // SLAB
    tile = (slabs, local * nx, SLAB)
    kin_band = pltpu.VMEM((2 * (2 * kin_reach + 1) * SLAB, SLAB), BF16)
    mag_band = (2 * (2 * reach + 1) * SLAB, SLAB)
    xf, xb, bwd_m, u_hi, u_lo, acc, sides, gpot = pl.pallas_call(
        functools.partial(exchange_kernel, devices, parts),
        out_shape=(
            shaped((nx, 3 * nx), BF16),
            shaped((nx, 3 * nx), BF16),
            shaped(mag_band, BF16),
            shaped(tile, BF16),
            shaped(tile, BF16),
            shaped((q_count, local * nx, LANES)),
            shaped((8, LANES)),
            shaped((devices, rows_per + 8, LANES)),
        ),
        in_specs=[HBM] * 7,
        out_specs=(VMEM,) * 8,
        scratch_shapes=[
            pltpu.VMEM((parts, nx, 3 * nx // parts), BF16), kin_band, pltpu.VMEM(mag_band, BF16),
            pltpu.VMEM(tile, BF16), pltpu.VMEM(tile, BF16), pltpu.VMEM(whole, F32),
            pltpu.VMEM((slot_each, nx, cells), F32), pltpu.VMEM(whole, F32),
            pltpu.VMEM(flat, F32), pltpu.VMEM(flat, F32), pltpu.VMEM(whole, F32), pltpu.VMEM(whole, F32),
            pltpu.VMEM((2, rows_per + 8, LANES), F32), pltpu.VMEM((functions, 3 * functions), BF16),
            pltpu.VMEM((functions, functions), F32), pltpu.VMEM((rows_per, LANES), F32),
            pltpu.VMEM((rows, LANES), F32), pltpu.VMEM((rows, LANES), F32),
            pltpu.SMEM(region_shift.shape, jnp.int32), pltpu.SMEM(owner_counts.shape, jnp.int32),
            pltpu.SMEM(kinetic_taps.shape, F32), pltpu.SMEM(magic_taps.shape, F32),
            pltpu.SemaphoreType.DMA((slot_each + 6,)), pltpu.SemaphoreType.DMA((2,)), each, each,
        ] + [each_part] * 6,
        compiler_params=params(collective_id=0),
        name="exchange",
    )(*(pltpu.with_memory_space_constraint(x, pltpu.HBM) for x in (
        support_functions, region_shift, owner_counts, kernel, external.reshape(rows_per, LANES),
        kinetic_taps, magic_taps,
    )))

    return pl.pallas_call(
        functools.partial(filter_kernel, devices, rows_per),
        out_shape=shaped((local, nx, cells)),
        in_specs=[VMEM] * 8,
        out_specs=HBM,
        scratch_shapes=[
            pltpu.VMEM(tile, BF16), pltpu.VMEM(tile, BF16), pltpu.VMEM((local, nx, cells), F32),
            pltpu.SemaphoreType.DMA((slabs // 2 + 1,)),
        ],
        compiler_params=params(),
        name="filter",
    )(u_hi, u_lo, acc, sides, gpot.reshape(-1, LANES), xf, xb, bwd_m)


def solution(mesh):
    placed = (P("fn", None, None), P(), P("fn"), P(), P("fn"), P(), P())
    return jax.shard_map(
        body, mesh=mesh, in_specs=placed, out_specs=P("fn", None, None), check_vma=False
    )
```
